32 devices in a mesh: parts: 2 (over x), gy: 16 (over z, y, core).
Axes of the slice: x: 2, y: 2, z: 4, core: 2. Of those that a mesh axis runs over, the one named last changes fastest.
Arguments:
- zero_filled: float32 [32, 2, 64, 128], P(('parts', 'gy')), parts along dimension 0, may hold values from -6 to 6
- coil_maps: bfloat16 [32, 2, 32, 64, 128], P(('parts', 'gy')), parts along dimension 0, may hold values from -0.75 to 0.75
- offsets: int32 [128], P('parts'), parts along dimension 0, may hold values from 0 to 3
- step_sizes: float32 [1], replicated, may hold values from 0.6 to 1.4
- w_in: bfloat16 [64, 2, 3, 3], replicated, may hold values from -1.5 to 1.5
- b_in: float32 [64], replicated, may hold values from -0.5 to 0.5
- w_mid: bfloat16 [64, 64, 3, 3], replicated, may hold values from -0.25 to 0.25
- b_mid: float32 [64], replicated, may hold values from -0.5 to 0.5
- w_out: bfloat16 [2, 64, 3, 3], replicated, may hold values from -0.125 to 0.125
- b_out: float32 [2], replicated, may hold values from -0.5 to 0.5
Outputs:
- recon: float32 [32, 2, 64, 128], P(('parts', 'gy')), parts along dimension 0
The draws below stay inside these ranges and needn't reach their ends.
There are 2 independent parts, one for each index of `parts`. The reference program is written for one: setup_inputs(seed, part) draws one part's arguments, and reference() takes and returns one part's arrays. A program takes and returns all parts, laid end to end along the dimension named above; an argument that names none is the same for every part. Nothing has to cross between parts.
Inputs may be any that keep to these rules, and one draw needn't show every extreme that they name: Readout row x samples the phase-encode lines offsets[x] + 4 m.
All inputs are finite; a program needn't handle non-finite values.
Results may differ from the reference program's by a relative error of at most 0.0012.
Values may be sent and summed in bfloat16 or wider, within the bound.
No kernel may reach another device: no remote copies, remote signals or barrier semaphores. Data moves between devices by JAX's collectives and lax.ppermute only.
A program may use at most 64 MiB of HBM per device.

```python
import jax
import jax.numpy as jnp
from jax import lax

X = 64
Z = 128
C = 32
CH = 64
ITERS = 1
NY = 16


def with_ends(array, key, low, top_value):
    shape = array.shape
    spot = [jax.random.randint(jax.random.fold_in(key, axis), (), 0, shape[axis]) for axis in range(len(shape))]
    array = array.at[tuple(spot)].set(low)
    longest = shape.index(max(shape))
    spot[longest] = (spot[longest] + 1) % shape[longest]
    return array.at[tuple(spot)].set(top_value)


def shard_levels(key, shape, pieces, low, largest):
    level = 1.0
    for position, shards_of in pieces:
        heights = jax.random.uniform(jax.random.fold_in(jax.random.fold_in(key, 6), position), (shards_of,), jnp.float32, low / len(pieces), largest / len(pieces))
        level = level * jnp.repeat(jnp.exp(heights), shape[position] // shards_of).reshape((-1,) + (1,) * (len(shape) - 1 - position))
    return level


def centred(key, dims, deviation, reach, shards=(), kind=jnp.bfloat16):
    entries = deviation * jax.random.normal(key, dims, jnp.float32)
    if shards:
        entries = entries * shard_levels(key, dims, shards, -0.22, 0.18)
    return jnp.clip(entries, -reach, reach).astype(kind)


def setup_inputs(seed: int = 0, part: int = 0) -> dict:
    seeds = jax.random.split(jax.random.key(seed), 11)
    part_splits = jax.random.split(jax.random.fold_in(seeds[10], part), 11)
    zero_filled = centred(part_splits[0], (NY, 2, X, Z), 1.0, 6.0, ((0, 16),), jnp.float32)
    coil_maps = centred(part_splits[1], (NY, 2, C, X, Z), (2 * C) ** -0.5, 0.75, ((0, 16),))
    offsets = with_ends(jax.random.randint(part_splits[2], (X,), 0, 4), jax.random.fold_in(part_splits[2], 1), 0, 3).astype(jnp.int32)
    step_sizes = jnp.clip(jax.random.uniform(seeds[3], (ITERS,), jnp.float32, 0.6, 1.4), 0.6, 1.4)
    w_in = centred(seeds[4], (CH, 2, 3, 3), 18 ** -0.5, 1.5)
    b_in = jnp.clip(jax.random.uniform(seeds[5], (CH,), jnp.float32, -0.5, 0.5), -0.5, 0.5)
    w_mid = centred(seeds[6], (CH, CH, 3, 3), (9 * CH) ** -0.5, 0.25)
    b_mid = jnp.clip(jax.random.uniform(seeds[7], (CH,), jnp.float32, -0.5, 0.5), -0.5, 0.5)
    w_out = centred(seeds[8], (2, CH, 3, 3), (36 * CH) ** -0.5, 0.125)
    b_out = jnp.clip(jax.random.uniform(seeds[9], (2,), jnp.float32, -0.5, 0.5), -0.5, 0.5)
    return dict(zero_filled=zero_filled, coil_maps=coil_maps, offsets=offsets, step_sizes=step_sizes, w_in=w_in, b_in=b_in, w_mid=w_mid, b_mid=b_mid, w_out=w_out, b_out=b_out)


def phase_tables(offsets):
    turns = (jnp.arange(4, dtype=jnp.int32)[:, None] * offsets[None, :]) % 4
    cosines = (turns == 0).astype(jnp.float32) - (turns == 2).astype(jnp.float32)
    sines = (turns == 3).astype(jnp.float32) - (turns == 1).astype(jnp.float32)
    return cosines, sines


def fold_normal(maps_list, field_list, cosines, sines):
    folded_real = None
    folded_imag = None
    for partner in range(4):
        maps_real = maps_list[partner][:, 0].astype(jnp.float32)
        maps_imag = maps_list[partner][:, 1].astype(jnp.float32)
        field_real = field_list[partner][:, 0][:, None]
        field_imag = field_list[partner][:, 1][:, None]
        coil_real = maps_real * field_real - maps_imag * field_imag
        coil_imag = maps_real * field_imag + maps_imag * field_real
        cosine = cosines[partner][None, None, :, None]
        sine = sines[partner][None, None, :, None]
        term_real = cosine * coil_real - sine * coil_imag
        term_imag = cosine * coil_imag + sine * coil_real
        if partner == 0:
            folded_real, folded_imag = term_real, term_imag
        else:
            folded_real = folded_real + term_real
            folded_imag = folded_imag + term_imag
    folded_real = 0.25 * folded_real
    folded_imag = 0.25 * folded_imag
    own_real = maps_list[0][:, 0].astype(jnp.float32)
    own_imag = maps_list[0][:, 1].astype(jnp.float32)
    normal_real = jnp.sum(own_real * folded_real + own_imag * folded_imag, axis=1)
    normal_imag = jnp.sum(own_real * folded_imag - own_imag * folded_real, axis=1)
    return jnp.stack([normal_real, normal_imag], axis=1)


def convolve(inputs, kernel):
    return lax.conv_general_dilated(inputs, kernel, (1, 1), "SAME", dimension_numbers=("NCHW", "OIHW", "NCHW"), preferred_element_type=jnp.float32)


def denoise(stepped, w_in, b_in, w_mid, b_mid, w_out, b_out):
    stepped_low = stepped.astype(jnp.bfloat16)
    hidden_one = jax.nn.relu(convolve(stepped_low, w_in) + b_in[None, :, None, None]).astype(jnp.bfloat16)
    hidden_two = jax.nn.relu(convolve(hidden_one, w_mid) + b_mid[None, :, None, None]).astype(jnp.bfloat16)
    return stepped + convolve(hidden_two, w_out) + b_out[None, :, None, None]


def reference(zero_filled, coil_maps, offsets, step_sizes, w_in, b_in, w_mid, b_mid, w_out, b_out):
    cosines, sines = phase_tables(offsets)
    quarter = zero_filled.shape[0] // 4
    maps_list = [jnp.roll(coil_maps, -partner * quarter, axis=0) for partner in range(4)]
    field = zero_filled
    for turn in range(ITERS):
        field_list = [jnp.roll(field, -partner * quarter, axis=0) for partner in range(4)]
        normal = fold_normal(maps_list, field_list, cosines, sines)
        stepped = field - step_sizes[turn] * (normal - zero_filled)
        field = denoise(stepped, w_in, b_in, w_mid, b_mid, w_out, b_out)
    return field
```

```python
import functools

import jax
import jax.numpy as jnp
from jax import lax
from jax.experimental import pallas as pl
from jax.experimental.pallas import tpu as pltpu
from jax.sharding import PartitionSpec as P

FOLDS = 4
GROUP = 16
QUAD = 4
PAD = 8

VMEM = pl.BlockSpec(memory_space=pltpu.VMEM)
SMEM = pl.BlockSpec(memory_space=pltpu.SMEM)


def fold_kernel(share_ref, maps_ref, field_ref, one_ref, two_ref, three_ref, offs_ref, out0, out1, out2, out3):
    coils = maps_ref.shape[2]
    offs = offs_ref[...]
    pieces = (None, one_ref, two_ref, three_ref)
    outs = (out0, out1, out2, out3)
    turned = []
    units = []
    for k in range(FOLDS):
        if k == 0:
            real, imag = field_ref[0, 0], field_ref[0, 1]
            turned.append((real, imag))
            units.append(None)
            continue
        piece = pieces[k]
        real = piece[0, coils].astype(jnp.float32) + piece[0, coils + 1].astype(jnp.float32)
        imag = piece[1, coils].astype(jnp.float32) + piece[1, coils + 1].astype(jnp.float32)
        turns = (k * offs) & 3
        zero, one = jnp.zeros_like(real), jnp.ones_like(real)
        cosine = jnp.where(turns == 0, one, jnp.where(turns == 2, -one, zero))
        sine = jnp.where(turns == 1, one, jnp.where(turns == 3, -one, zero))
        units.append((cosine, sine))
        turned.append((cosine * real - sine * imag, cosine * imag + sine * real))

    def step(c, sums):
        maps = []
        fold_real = fold_imag = None
        for k in range(FOLDS):
            if k == 0:
                real, imag = maps_ref[0, 0, c], maps_ref[0, 1, c]
            else:
                real, imag = pieces[k][0, c], pieces[k][1, c]
            real, imag = real.astype(jnp.float32), imag.astype(jnp.float32)
            maps.append((real, imag))
            term_real = real * turned[k][0] - imag * turned[k][1]
            term_imag = real * turned[k][1] + imag * turned[k][0]
            fold_real = term_real if k == 0 else fold_real + term_real
            fold_imag = term_imag if k == 0 else fold_imag + term_imag
        new = []
        for k in range(FOLDS):
            real, imag = maps[k]
            new.append(sums[2 * k] + (real * fold_real + imag * fold_imag))
            new.append(sums[2 * k + 1] + (real * fold_imag - imag * fold_real))
        return tuple(new)

    zeros = tuple(jnp.zeros(offs.shape, jnp.float32) for _ in range(2 * FOLDS))
    sums = lax.fori_loop(0, coils, step, zeros, unroll=4)
    for k in range(FOLDS):
        real, imag = 0.25 * sums[2 * k], 0.25 * sums[2 * k + 1]
        if k == 0:
            outs[k][0], outs[k][1] = real, imag
        else:
            cosine, sine = units[k]
            outs[k][0] = cosine * real + sine * imag
            outs[k][1] = cosine * imag - sine * real


def fold(share, coil_maps, field, pieces, offs):
    _, _, coils, _, z = coil_maps.shape
    rows = offs.shape[0]
    whole = lambda *shape: pl.BlockSpec(shape, lambda i, s: (0,) * len(shape))
    spec = pltpu.PrefetchScalarGridSpec(
        num_scalar_prefetch=1,
        grid=(1,),
        in_specs=[
            pl.BlockSpec((1, 2, coils, rows, z), lambda i, s: (0, 0, 0, s[0], 0)),
            pl.BlockSpec((1, 2, rows, z), lambda i, s: (0, 0, s[0], 0)),
            whole(*pieces[0].shape),
            whole(*pieces[1].shape),
            whole(*pieces[2].shape),
            whole(rows, z),
        ],
        out_specs=[whole(2, rows, z)] * FOLDS,
    )
    return pl.pallas_call(
        fold_kernel,
        grid_spec=spec,
        out_shape=[jax.ShapeDtypeStruct((2, rows, z), jnp.float32)] * FOLDS,
        cost_estimate=pl.CostEstimate(flops=70 * coils * rows * z, bytes_accessed=16 * coils * rows * z, transcendentals=0),
        name="fold",
    )(share, coil_maps, field, *pieces, offs)


def shifted(value, lane, tap, width):
    if tap == 1:
        return value
    if tap == 0:
        return jnp.where(lane == 0, 0.0, pltpu.roll(value, 1, 1))
    return jnp.where(lane == width - 1, 0.0, pltpu.roll(value, width - 1, 1))


def denoise_kernel(
    share_ref, step_ref, tail_ref, field_ref, own_ref, one_ref, two_ref, three_ref,
    w1_ref, b1_ref, w2_ref, b2_ref, w3_ref, out_ref, padded, window, low, hidden_one, hidden_two,
):
    _, _, x_size, z = field_ref.shape
    rows = own_ref.shape[1]
    ch = b1_ref.shape[0]
    share = share_ref[0]
    step = step_ref[0]
    groups = x_size // GROUP
    for k, ref in enumerate((own_ref, one_ref, two_ref, three_ref)):
        start = pl.multiple_of(((share + k) % FOLDS) * rows, rows)
        for part in range(2):
            padded[part, pl.ds(PAD + start, rows), :] = ref[part]
    edge = jnp.zeros((PAD, z), jnp.float32)
    for part in range(2):
        padded[part, 0:PAD, :] = edge
        padded[part, PAD + x_size : PAD + x_size + PAD, :] = edge
        base = field_ref[0, part]
        stepped = base - step * (padded[part, PAD : PAD + x_size, :] - base)
        padded[part, PAD : PAD + x_size, :] = stepped
    lane = lax.broadcasted_iota(jnp.int32, (x_size + 2 * PAD, z), 1)
    for tap in range(3):
        for part in range(2):
            window[tap, part] = shifted(padded[part], lane, tap, z).astype(jnp.bfloat16)
    span = GROUP + 2 * PAD
    for g in range(groups):
        for tap in range(3):
            for part in range(2):
                low[(tap * 2 + part) * span : (tap * 2 + part + 1) * span, g * z : (g + 1) * z] = window[
                    tap, part, g * GROUP : g * GROUP + span, :
                ]
    empty = jnp.zeros((ch, z), jnp.bfloat16)
    for tap in range(3):
        hidden_one[tap, 0:ch, :] = empty
        hidden_one[tap, (x_size + 1) * ch : (x_size + 2) * ch, :] = empty
    hidden_two[0:ch, :] = empty
    hidden_two[(x_size + 1) * ch : (x_size + 2) * ch, :] = empty

    lane = lax.broadcasted_iota(jnp.int32, (ch, z), 1)
    bias = b1_ref[...]
    for r in range(0, GROUP, QUAD):
        for g in range(0, groups, 2):
            out = jnp.dot(
                w1_ref[r * ch : (r + QUAD) * ch, :], low[:, g * z : (g + 2) * z], preferred_element_type=jnp.float32
            )
            for i in range(QUAD):
                for j in range(2):
                    value = jnp.maximum(out[i * ch : (i + 1) * ch, j * z : (j + 1) * z] + bias, 0.0)
                    row = (g + j) * GROUP + r + i + 1
                    for tap in range(3):
                        hidden_one[tap, row * ch : (row + 1) * ch, :] = shifted(value, lane, tap, z).astype(jnp.bfloat16)

    bias = b2_ref[...]
    half = x_size // 2
    for q in range(0, half, QUAD):
        column = lambda first: jnp.concatenate(
            [hidden_one[tap, first * ch : (first + QUAD + 2) * ch, :] for tap in range(3)], axis=0
        )
        out = jnp.dot(
            w2_ref[...], jnp.concatenate([column(q), column(q + half)], axis=1), preferred_element_type=jnp.float32
        )
        for i in range(QUAD):
            for j in range(2):
                value = jnp.maximum(out[i * ch : (i + 1) * ch, j * z : (j + 1) * z] + bias, 0.0)
                row = q + j * half + i + 1
                hidden_two[row * ch : (row + 1) * ch, :] = value.astype(jnp.bfloat16)

    lane = lax.broadcasted_iota(jnp.int32, (2 * GROUP, z), 1)
    for g in range(0, groups, 2):
        column = lambda first: hidden_two[first * GROUP * ch : (first * GROUP + GROUP + 2) * ch, :]
        out = jnp.dot(
            w3_ref[...], jnp.concatenate([column(g), column(g + 1)], axis=1), preferred_element_type=jnp.float32
        )
        for j in range(2):
            total = None
            for tap in range(3):
                part = out[tap * 2 * GROUP : (tap + 1) * 2 * GROUP, j * z : (j + 1) * z]
                part = shifted(part, lane, tap, z)
                total = part if total is None else total + part
            first = (g + j) * GROUP
            for part in range(2):
                out_ref[0, part, first : first + GROUP, :] = (
                    padded[part, PAD + first : PAD + first + GROUP, :]
                    + total[part * GROUP : (part + 1) * GROUP]
                    + tail_ref[part]
                )


def denoise(share, step, field, normals, weights):
    _, _, x_size, z = field.shape
    w1, b1, w2, b2, w3, b_out = weights
    ch = b1.shape[0]
    span = GROUP + 2 * PAD
    return pl.pallas_call(
        denoise_kernel,
        in_specs=[SMEM, SMEM, SMEM] + [VMEM] * 10,
        out_specs=VMEM,
        out_shape=jax.ShapeDtypeStruct(field.shape, jnp.float32),
        scratch_shapes=[
            pltpu.VMEM((2, x_size + 2 * PAD, z), jnp.float32),
            pltpu.VMEM((3, 2, x_size + 2 * PAD, z), jnp.bfloat16),
            pltpu.VMEM((6 * span, x_size // GROUP * z), jnp.bfloat16),
            pltpu.VMEM((3, (x_size + 2) * ch, z), jnp.bfloat16),
            pltpu.VMEM(((x_size + 2) * ch, z), jnp.bfloat16),
        ],
        cost_estimate=pl.CostEstimate(flops=4_000_000_000, bytes_accessed=2_000_000, transcendentals=0),
        name="denoise",
    )(share, step, b_out, field, *normals, w1, b1, w2, b2, w3)


def banded(kernel, axis, copies, length, first, at):
    taps = kernel.shape[axis]
    rows = []
    for r in range(copies):
        pads = [(0, 0)] * kernel.ndim
        pads[axis] = (r + first, length - taps - r - first)
        rows.append(jnp.pad(kernel, pads))
    return jnp.stack(rows, axis=at)


def prepare(w_in, b_in, w_mid, b_mid, w_out, b_out, z):
    ch = w_mid.shape[0]
    span = GROUP + 2 * PAD
    w1 = banded(w_in.transpose(0, 3, 1, 2), 3, GROUP, span, PAD - 1, 0).reshape(GROUP * ch, 6 * span)
    w2 = banded(w_mid.transpose(0, 3, 2, 1), 2, QUAD, QUAD + 2, 0, 0).reshape(QUAD * ch, 3 * (QUAD + 2) * ch)
    w3 = banded(w_out.transpose(3, 0, 2, 1), 2, GROUP, GROUP + 2, 0, 2).reshape(6 * GROUP, (GROUP + 2) * ch)
    b1 = jnp.broadcast_to(b_in[:, None], (ch, z))
    b2 = jnp.broadcast_to(b_mid[:, None], (ch, z))
    return w1, b1, w2, b2, w3, b_out


def per_device(zero_filled, coil_maps, offsets, step_sizes, w_in, b_in, w_mid, b_mid, w_out, b_out):
    devices = lax.axis_size("gy")
    stride = devices // FOLDS
    x_size, z = zero_filled.shape[2:]
    rows = x_size // FOLDS
    share = lax.axis_index("gy") // stride

    def pairs(k):
        return [(j, (j + k * stride) % devices) for j in range(devices)]

    high = lax.reduce_precision(zero_filled[0], exponent_bits=8, mantissa_bits=7)
    split = jnp.stack([high.astype(jnp.bfloat16), (zero_filled[0] - high).astype(jnp.bfloat16)], axis=1)
    pieces = []
    for k in range(1, FOLDS):
        first = ((share + k) % FOLDS) * rows
        piece = jnp.concatenate(
            [
                lax.dynamic_slice_in_dim(coil_maps[0], first, rows, 2),
                lax.dynamic_slice_in_dim(split, first, rows, 2),
            ],
            axis=1,
        )
        pieces.append(lax.ppermute(piece, "gy", pairs(k)))
    weights = prepare(w_in, b_in, w_mid, b_mid, w_out, b_out, z)
    offs = lax.dynamic_slice_in_dim(offsets, share * rows, rows, 0)
    offs = jnp.broadcast_to(offs[:, None], (rows, z))
    index = jnp.reshape(share, (1,)).astype(jnp.int32)
    normals = fold(index, coil_maps, zero_filled, pieces, offs)
    normals = [normals[0]] + [lax.ppermute(normals[k], "gy", pairs(-k)) for k in range(1, FOLDS)]
    return denoise(index, step_sizes, zero_filled, normals, weights)


def solution(mesh):
    in_specs = (
        P(("parts", "gy"), None, None, None),
        P(("parts", "gy"), None, None, None, None),
        P("parts"),
        P(),
        P(),
        P(),
        P(),
        P(),
        P(),
        P(),
    )
    out_specs = P(("parts", "gy"), None, None, None)
    return jax.shard_map(
        per_device, mesh=mesh, in_specs=in_specs, out_specs=out_specs, check_vma=False
    )
```

```python
import jax
import jax.numpy as jnp
from jax import lax
from jax.experimental import pallas as pl
from jax.experimental.pallas import tpu as pltpu
from jax.sharding import PartitionSpec as P

FOLDS = 4
GROUP = 16
QUAD = 4
PAIR = 2
PAD = 8

VMEM = pl.BlockSpec(memory_space=pltpu.VMEM)
SMEM = pl.BlockSpec(memory_space=pltpu.SMEM)


def fold_kernel(share_ref, maps_ref, field_ref, one_ref, two_ref, three_ref, offs_ref, out0, out1, out2, out3):
    coils = maps_ref.shape[2]
    share = share_ref[0]
    offs = offs_ref[...]
    pieces = (None, one_ref, two_ref, three_ref)
    outs = (out0, out1, out2, out3)
    turned = []
    units = []
    for k in range(FOLDS):
        if k == 0:
            real, imag = field_ref[0, 0], field_ref[0, 1]
            turned.append((real, imag))
            units.append(None)
            continue
        piece = pieces[k]
        real = piece[0, coils].astype(jnp.float32) + piece[0, coils + 1].astype(jnp.float32)
        imag = piece[1, coils].astype(jnp.float32) + piece[1, coils + 1].astype(jnp.float32)
        turns = (((share ^ k) - share) * offs) & 3
        zero, one = jnp.zeros_like(real), jnp.ones_like(real)
        cosine = jnp.where(turns == 0, one, jnp.where(turns == 2, -one, zero))
        sine = jnp.where(turns == 3, one, jnp.where(turns == 1, -one, zero))
        units.append((cosine, sine))
        turned.append((cosine * real - sine * imag, cosine * imag + sine * real))

    def step(c, sums):
        maps = []
        fold_real = fold_imag = None
        for k in range(FOLDS):
            if k == 0:
                real, imag = maps_ref[0, 0, c], maps_ref[0, 1, c]
            else:
                real, imag = pieces[k][0, c], pieces[k][1, c]
            real, imag = real.astype(jnp.float32), imag.astype(jnp.float32)
            maps.append((real, imag))
            term_real = real * turned[k][0] - imag * turned[k][1]
            term_imag = real * turned[k][1] + imag * turned[k][0]
            fold_real = term_real if k == 0 else fold_real + term_real
            fold_imag = term_imag if k == 0 else fold_imag + term_imag
        new = []
        for k in range(FOLDS):
            real, imag = maps[k]
            new.append(sums[2 * k] + (real * fold_real + imag * fold_imag))
            new.append(sums[2 * k + 1] + (real * fold_imag - imag * fold_real))
        return tuple(new)

    zeros = tuple(jnp.zeros(offs.shape, jnp.float32) for _ in range(2 * FOLDS))
    sums = lax.fori_loop(0, coils, step, zeros, unroll=4)
    for k in range(FOLDS):
        real, imag = 0.25 * sums[2 * k], 0.25 * sums[2 * k + 1]
        if k == 0:
            outs[k][0], outs[k][1] = real, imag
        else:
            cosine, sine = units[k]
            outs[k][0] = cosine * real + sine * imag
            outs[k][1] = cosine * imag - sine * real


def fold(share, coil_maps, field, pieces, offs):
    _, _, coils, _, z = coil_maps.shape
    rows = offs.shape[0]
    whole = lambda *shape: pl.BlockSpec(shape, lambda i, s: (0,) * len(shape))
    spec = pltpu.PrefetchScalarGridSpec(
        num_scalar_prefetch=1,
        grid=(1,),
        in_specs=[
            pl.BlockSpec((1, 2, coils, rows, z), lambda i, s: (0, 0, 0, s[0], 0)),
            pl.BlockSpec((1, 2, rows, z), lambda i, s: (0, 0, s[0], 0)),
            whole(*pieces[0].shape),
            whole(*pieces[1].shape),
            whole(*pieces[2].shape),
            whole(rows, z),
        ],
        out_specs=[whole(2, rows, z)] * FOLDS,
    )
    return pl.pallas_call(
        fold_kernel,
        grid_spec=spec,
        out_shape=[jax.ShapeDtypeStruct((2, rows, z), jnp.float32)] * FOLDS,
        cost_estimate=pl.CostEstimate(flops=70 * coils * rows * z, bytes_accessed=16 * coils * rows * z, transcendentals=0),
        compiler_params=pltpu.CompilerParams(vmem_limit_bytes=8 << 20),
        name="fold",
    )(share, coil_maps, field, *pieces, offs)


def shifted(value, lane, tap, width):
    if tap == 1:
        return value
    if tap == 0:
        return jnp.where(lane == 0, 0.0, pltpu.roll(value, 1, 1))
    return jnp.where(lane == width - 1, 0.0, pltpu.roll(value, width - 1, 1))


def denoise_kernel(
    share_ref, step_ref, tail_ref, field_ref, own_ref, one_ref, two_ref, three_ref,
    w1_ref, b1_ref, w2_ref, b2_ref, w3_ref, out_ref, padded, window, low, hidden_one, hidden_two,
):
    _, _, x_size, z = field_ref.shape
    rows = own_ref.shape[1]
    ch = b1_ref.shape[0]
    share = share_ref[0]
    step = step_ref[0]
    groups = x_size // GROUP
    for k, ref in enumerate((own_ref, one_ref, two_ref, three_ref)):
        start = pl.multiple_of((share ^ k) * rows, rows)
        for part in range(2):
            padded[part, pl.ds(PAD + start, rows), :] = ref[part]
    edge = jnp.zeros((PAD, z), jnp.float32)
    for part in range(2):
        padded[part, 0:PAD, :] = edge
        padded[part, PAD + x_size : PAD + x_size + PAD, :] = edge
        base = field_ref[0, part]
        stepped = base - step * (padded[part, PAD : PAD + x_size, :] - base)
        padded[part, PAD : PAD + x_size, :] = stepped
    lane = lax.broadcasted_iota(jnp.int32, (x_size + 2 * PAD, z), 1)
    for tap in range(3):
        for part in range(2):
            window[tap, part] = shifted(padded[part], lane, tap, z).astype(jnp.bfloat16)
    span = GROUP + 2 * PAD
    for g in range(groups):
        for tap in range(3):
            for part in range(2):
                low[(tap * 2 + part) * span : (tap * 2 + part + 1) * span, g * z : (g + 1) * z] = window[
                    tap, part, g * GROUP : g * GROUP + span, :
                ]
    empty = jnp.zeros((ch, z), jnp.bfloat16)
    for hidden in (hidden_one, hidden_two):
        hidden[0:ch, :] = empty
        hidden[(x_size + 1) * ch : (x_size + 2) * ch, :] = empty

    bias = b1_ref[...]
    for r in range(0, GROUP, QUAD):
        for g in range(0, groups, 2):
            out = jnp.dot(
                w1_ref[r * ch : (r + QUAD) * ch, :], low[:, g * z : (g + 2) * z], preferred_element_type=jnp.float32
            )
            for i in range(QUAD):
                for j in range(2):
                    value = jnp.maximum(out[i * ch : (i + 1) * ch, j * z : (j + 1) * z] + bias, 0.0)
                    row = (g + j) * GROUP + r + i + 1
                    hidden_one[row * ch : (row + 1) * ch, :] = value.astype(jnp.bfloat16)

    bias = b2_ref[...]
    lane = lax.broadcasted_iota(jnp.int32, (ch, z), 1)
    half = x_size // 2
    for q in range(0, half, PAIR):
        column = lambda first: hidden_one[first * ch : (first + PAIR + 2) * ch, :]
        out = jnp.dot(
            w2_ref[...], jnp.concatenate([column(q), column(q + half)], axis=1), preferred_element_type=jnp.float32
        )
        for i in range(PAIR):
            for j in range(2):
                total = bias
                for tap in range(3):
                    first = (tap * PAIR + i) * ch
                    total = total + shifted(out[first : first + ch, j * z : (j + 1) * z], lane, tap, z)
                row = q + j * half + i + 1
                hidden_two[row * ch : (row + 1) * ch, :] = jnp.maximum(total, 0.0).astype(jnp.bfloat16)

    lane = lax.broadcasted_iota(jnp.int32, (2 * GROUP, z), 1)
    for g in range(0, groups, 2):
        column = lambda first: hidden_two[first * GROUP * ch : (first * GROUP + GROUP + 2) * ch, :]
        out = jnp.dot(
            w3_ref[...], jnp.concatenate([column(g), column(g + 1)], axis=1), preferred_element_type=jnp.float32
        )
        for j in range(2):
            total = None
            for tap in range(3):
                part = out[tap * 2 * GROUP : (tap + 1) * 2 * GROUP, j * z : (j + 1) * z]
                part = shifted(part, lane, tap, z)
                total = part if total is None else total + part
            first = (g + j) * GROUP
            for part in range(2):
                out_ref[0, part, first : first + GROUP, :] = (
                    padded[part, PAD + first : PAD + first + GROUP, :]
                    + total[part * GROUP : (part + 1) * GROUP]
                    + tail_ref[part]
                )


def denoise(share, step, field, normals, weights, b_out):
    _, _, x_size, z = field.shape
    w1, b1, w2, b2, w3 = weights
    ch = b1.shape[0]
    span = GROUP + 2 * PAD
    return pl.pallas_call(
        denoise_kernel,
        in_specs=[SMEM, SMEM, SMEM] + [VMEM] * 10,
        out_specs=VMEM,
        out_shape=jax.ShapeDtypeStruct(field.shape, jnp.float32),
        scratch_shapes=[
            pltpu.VMEM((2, x_size + 2 * PAD, z), jnp.float32),
            pltpu.VMEM((3, 2, x_size + 2 * PAD, z), jnp.bfloat16),
            pltpu.VMEM((6 * span, x_size // GROUP * z), jnp.bfloat16),
            pltpu.VMEM(((x_size + 2) * ch, z), jnp.bfloat16),
            pltpu.VMEM(((x_size + 2) * ch, z), jnp.bfloat16),
        ],
        cost_estimate=pl.CostEstimate(flops=4_000_000_000, bytes_accessed=2_000_000, transcendentals=0),
        compiler_params=pltpu.CompilerParams(vmem_limit_bytes=16 << 20),
        name="denoise",
    )(share, step, b_out, field, *normals, w1, b1, w2, b2, w3)


def prepare_kernel(w_in_ref, b_in_ref, w_mid_ref, b_mid_ref, w_out_ref, w1_ref, b1_ref, w2_ref, b2_ref, w3_ref):
    ch, z = b1_ref.shape
    span = GROUP + 2 * PAD
    b1_ref[...] = jnp.transpose(jnp.broadcast_to(b_in_ref[...], (z, ch)))
    b2_ref[...] = jnp.transpose(jnp.broadcast_to(b_mid_ref[...], (z, ch)))
    taps = w_in_ref[...]
    row = lax.broadcasted_iota(jnp.int32, (18, 6 * span), 0)
    column = lax.broadcasted_iota(jnp.int32, (18, 6 * span), 1)
    place = (row % 6) * span + row // 6 + (PAD - 1)
    for r in range(GROUP):
        select = jnp.where(column == place + r, 1.0, 0.0).astype(jnp.bfloat16)
        w1_ref[r * ch : (r + 1) * ch, :] = lax.dot_general(
            taps, select, (((0,), (0,)), ((), ())), preferred_element_type=jnp.float32
        ).astype(jnp.bfloat16)
    w2_ref[...] = jnp.zeros_like(w2_ref)
    for dz in range(3):
        for dx in range(3):
            block = w_mid_ref[dx, dz]
            for r in range(PAIR):
                first = (dz * PAIR + r) * ch
                w2_ref[first : first + ch, (r + dx) * ch : (r + dx + 1) * ch] = block
    wide = (GROUP, (GROUP + 2) * ch)
    offset = lax.broadcasted_iota(jnp.int32, wide, 1) // ch - lax.broadcasted_iota(jnp.int32, wide, 0)
    for dz in range(3):
        for part in range(2):
            total = jnp.zeros(wide, jnp.float32)
            for dx in range(3):
                line = w_out_ref[dx, dz, part : part + 1, :].astype(jnp.float32)
                line = jnp.concatenate([line] * (GROUP + 2), axis=1)
                total = jnp.where(offset == dx, jnp.broadcast_to(line, wide), total)
            first = (dz * 2 + part) * GROUP
            w3_ref[first : first + GROUP, :] = total.astype(jnp.bfloat16)


def prepare(w_in, b_in, w_mid, b_mid, w_out, z):
    ch = w_mid.shape[0]
    shapes = [
        jax.ShapeDtypeStruct((GROUP * ch, 6 * (GROUP + 2 * PAD)), jnp.bfloat16),
        jax.ShapeDtypeStruct((ch, z), jnp.float32),
        jax.ShapeDtypeStruct((3 * PAIR * ch, (PAIR + 2) * ch), jnp.bfloat16),
        jax.ShapeDtypeStruct((ch, z), jnp.float32),
        jax.ShapeDtypeStruct((6 * GROUP, (GROUP + 2) * ch), jnp.bfloat16),
    ]
    return pl.pallas_call(
        prepare_kernel,
        in_specs=[VMEM] * 5,
        out_specs=[VMEM] * 5,
        out_shape=shapes,
        cost_estimate=pl.CostEstimate(flops=1_000_000_000, bytes_accessed=8_000_000, transcendentals=0),
        compiler_params=pltpu.CompilerParams(vmem_limit_bytes=8 << 20),
        name="prepare",
    )(
        w_in.transpose(2, 3, 1, 0).reshape(18, ch),
        b_in[None],
        w_mid.transpose(2, 3, 0, 1),
        b_mid[None],
        w_out.transpose(2, 3, 0, 1),
    )


def pack_kernel(share_ref, maps_ref, field_ref, one_ref, two_ref, three_ref, sems):
    coils = maps_ref.shape[2]
    rows = one_ref.shape[2]
    copies = []
    for k, ref in ((2, two_ref), (1, one_ref), (3, three_ref)):
        first = pl.multiple_of((share_ref[0] ^ k) * rows, rows)
        for part in range(2):
            copy = pltpu.make_async_copy(
                maps_ref.at[0, part, :, pl.ds(first, rows), :], ref.at[part, 0:coils], sems.at[k - 1, part]
            )
            copy.start()
            copies.append(copy)
    for k, ref in ((2, two_ref), (1, one_ref), (3, three_ref)):
        first = pl.multiple_of((share_ref[0] ^ k) * rows, rows)
        for part in range(2):
            value = field_ref[0, part, pl.ds(first, rows), :]
            high = value.astype(jnp.bfloat16)
            ref[part, coils] = high
            ref[part, coils + 1] = (value - high.astype(jnp.float32)).astype(jnp.bfloat16)
    for copy in copies:
        copy.wait()


def pack(share, coil_maps, field):
    _, _, coils, x_size, z = coil_maps.shape
    piece = jax.ShapeDtypeStruct((2, coils + 2, x_size // FOLDS, z), jnp.bfloat16)
    return pl.pallas_call(
        pack_kernel,
        in_specs=[SMEM, pl.BlockSpec(memory_space=pltpu.HBM), VMEM],
        out_specs=[VMEM] * 3,
        out_shape=[piece] * 3,
        scratch_shapes=[pltpu.SemaphoreType.DMA((3, 2))],
        cost_estimate=pl.CostEstimate(flops=0, bytes_accessed=2_000_000, transcendentals=0),
        compiler_params=pltpu.CompilerParams(vmem_limit_bytes=4 << 20),
        name="pack",
    )(share, coil_maps, field)


def per_device(zero_filled, coil_maps, offsets, step_sizes, w_in, b_in, w_mid, b_mid, w_out, b_out):
    devices = lax.axis_size("gy")
    stride = devices // FOLDS
    x_size, z = zero_filled.shape[2:]
    rows = x_size // FOLDS
    share = lax.axis_index("gy") // stride

    def pairs(k):
        return [(j, (j // stride ^ k) * stride + j % stride) for j in range(devices)]

    index = jnp.reshape(share, (1,)).astype(jnp.int32)
    pieces = pack(index, coil_maps, zero_filled)
    pieces = {k: lax.ppermute(pieces[k - 1], "gy", pairs(k)) for k in (2, 3, 1)}
    pieces = [pieces[k] for k in range(1, FOLDS)]
    weights = prepare(w_in, b_in, w_mid, b_mid, w_out, z)
    offs = lax.dynamic_slice_in_dim(offsets, share * rows, rows, 0)
    offs = jnp.broadcast_to(offs[:, None], (rows, z))
    pieces, weights, offs = lax.optimization_barrier((pieces, weights, offs))
    normals = fold(index, coil_maps, zero_filled, pieces, offs)
    normals = [normals[0]] + [lax.ppermute(normals[k], "gy", pairs(k)) for k in range(1, FOLDS)]
    return denoise(index, step_sizes, zero_filled, normals, weights, b_out)


def solution(mesh):
    in_specs = (
        P(("parts", "gy"), None, None, None),
        P(("parts", "gy"), None, None, None, None),
        P("parts"),
        P(),
        P(),
        P(),
        P(),
        P(),
        P(),
        P(),
    )
    out_specs = P(("parts", "gy"), None, None, None)
    return jax.shard_map(
        per_device, mesh=mesh, in_specs=in_specs, out_specs=out_specs, check_vma=False
    )
```

```python
import functools

import jax
import jax.numpy as jnp
from jax import lax
from jax.experimental import pallas as pl
from jax.experimental.pallas import tpu as pltpu
from jax.sharding import PartitionSpec as P

FOLDS = 4
GROUP = 16
QUAD = 4
PAIR = 2
PAD = 8
ORDERS = ((2, 3, 1), (1, 2, 3))
PACK_LIMIT = 8 << 20

VMEM = pl.BlockSpec(memory_space=pltpu.VMEM)
HBM = pl.BlockSpec(memory_space=pltpu.HBM)
SMEM = pl.BlockSpec(memory_space=pltpu.SMEM)


def place(stride):
    position = lax.axis_index("gy")
    odd = position % 2
    return position // stride, [jnp.where(odd == 0, even, other) for even, other in zip(*ORDERS)]


def fold_kernel(stride, maps_ref, field_ref, one_ref, two_ref, three_ref, offs_ref, out0, out1, out2, out3):
    coils = maps_ref.shape[2]
    rows = out0.shape[1]
    share, distances = place(stride)
    own = pl.ds(pl.multiple_of(share * rows, rows), rows)
    offs = offs_ref[...]
    pieces = (None, one_ref, two_ref, three_ref)
    outs = (out0, out1, out2, out3)
    turned = []
    units = []
    for k in range(FOLDS):
        if k == 0:
            real, imag = field_ref[0, 0, own, :], field_ref[0, 1, own, :]
            turned.append((real, imag))
            units.append(None)
            continue
        piece = pieces[k]
        real = piece[0, coils].astype(jnp.float32) + piece[0, coils + 1].astype(jnp.float32)
        imag = piece[1, coils].astype(jnp.float32) + piece[1, coils + 1].astype(jnp.float32)
        turns = (((share ^ distances[k - 1]) - share) * offs) & 3
        zero, one = jnp.zeros_like(real), jnp.ones_like(real)
        cosine = jnp.where(turns == 0, one, jnp.where(turns == 2, -one, zero))
        sine = jnp.where(turns == 3, one, jnp.where(turns == 1, -one, zero))
        units.append((cosine, sine))
        turned.append((cosine * real - sine * imag, cosine * imag + sine * real))

    def step(c, sums):
        maps = []
        fold_real = fold_imag = None
        for k in range(FOLDS):
            if k == 0:
                real, imag = maps_ref[0, 0, c, own, :], maps_ref[0, 1, c, own, :]
            else:
                real, imag = pieces[k][0, c], pieces[k][1, c]
            real, imag = real.astype(jnp.float32), imag.astype(jnp.float32)
            maps.append((real, imag))
            term_real = real * turned[k][0] - imag * turned[k][1]
            term_imag = real * turned[k][1] + imag * turned[k][0]
            fold_real = term_real if k == 0 else fold_real + term_real
            fold_imag = term_imag if k == 0 else fold_imag + term_imag
        new = []
        for k in range(FOLDS):
            real, imag = maps[k]
            new.append(sums[2 * k] + (real * fold_real + imag * fold_imag))
            new.append(sums[2 * k + 1] + (real * fold_imag - imag * fold_real))
        return tuple(new)

    zeros = tuple(jnp.zeros(offs.shape, jnp.float32) for _ in range(2 * FOLDS))
    sums = lax.fori_loop(0, coils, step, zeros, unroll=8)
    for k in range(FOLDS):
        real, imag = 0.25 * sums[2 * k], 0.25 * sums[2 * k + 1]
        if k == 0:
            outs[k][0], outs[k][1] = real, imag
        else:
            cosine, sine = units[k]
            outs[k][0] = cosine * real + sine * imag
            outs[k][1] = cosine * imag - sine * real


def fold(stride, coil_maps, field, pieces, offs):
    coils = coil_maps.shape[2]
    rows, z = offs.shape
    return pl.pallas_call(
        functools.partial(fold_kernel, stride),
        in_specs=[VMEM] * 6,
        out_specs=[VMEM] * FOLDS,
        out_shape=[jax.ShapeDtypeStruct((2, rows, z), jnp.float32)] * FOLDS,
        cost_estimate=pl.CostEstimate(flops=70 * coils * rows * z, bytes_accessed=16 * coils * rows * z, transcendentals=0),
        compiler_params=pltpu.CompilerParams(vmem_limit_bytes=8 << 20),
        name="fold",
    )(coil_maps, field, *pieces, offs)


def shifted(value, lane, tap, width):
    if tap == 1:
        return value
    if tap == 0:
        return jnp.where(lane == 0, 0.0, pltpu.roll(value, 1, 1))
    return jnp.where(lane == width - 1, 0.0, pltpu.roll(value, width - 1, 1))


def denoise_kernel(
    stride, step_ref, tail_ref, field_ref, own_ref, one_ref, two_ref, three_ref,
    w1_ref, b1_ref, w2_ref, b2_ref, w3_ref, out_ref, padded, window, low, hidden_one, hidden_two,
):
    _, _, x_size, z = field_ref.shape
    rows = own_ref.shape[1]
    ch = b1_ref.shape[0]
    share, distances = place(stride)
    groups = x_size // GROUP
    for k, ref in enumerate((own_ref, one_ref, two_ref, three_ref)):
        start = pl.multiple_of((share if k == 0 else share ^ distances[k - 1]) * rows, rows)
        for part in range(2):
            padded[part, pl.ds(PAD + start, rows), :] = ref[part]
    edge = jnp.zeros((PAD, z), jnp.float32)
    for part in range(2):
        padded[part, 0:PAD, :] = edge
        padded[part, PAD + x_size : PAD + x_size + PAD, :] = edge
        base = field_ref[0, part]
        stepped = base - step_ref[...] * (padded[part, PAD : PAD + x_size, :] - base)
        padded[part, PAD : PAD + x_size, :] = stepped
    lane = lax.broadcasted_iota(jnp.int32, (x_size + 2 * PAD, z), 1)
    for tap in range(3):
        for part in range(2):
            window[tap, part] = shifted(padded[part], lane, tap, z).astype(jnp.bfloat16)
    span = GROUP + 2 * PAD
    for g in range(groups):
        for tap in range(3):
            for part in range(2):
                low[(tap * 2 + part) * span : (tap * 2 + part + 1) * span, g * z : (g + 1) * z] = window[
                    tap, part, g * GROUP : g * GROUP + span, :
                ]
    empty = jnp.zeros((ch, z), jnp.bfloat16)
    for hidden in (hidden_one, hidden_two):
        hidden[0:ch, :] = empty
        hidden[(x_size + 1) * ch : (x_size + 2) * ch, :] = empty

    bias = b1_ref[...]
    for r in range(0, GROUP, QUAD):
        for g in range(0, groups, 2):
            out = jnp.dot(
                w1_ref[r * ch : (r + QUAD) * ch, :], low[:, g * z : (g + 2) * z], preferred_element_type=jnp.float32
            )
            for i in range(QUAD):
                for j in range(2):
                    value = jnp.maximum(out[i * ch : (i + 1) * ch, j * z : (j + 1) * z] + bias, 0.0)
                    row = (g + j) * GROUP + r + i + 1
                    hidden_one[row * ch : (row + 1) * ch, :] = value.astype(jnp.bfloat16)

    bias = b2_ref[...]
    lane = lax.broadcasted_iota(jnp.int32, (ch, z), 1)
    half = x_size // 2
    for q in range(0, half, PAIR):
        column = lambda first: hidden_one[first * ch : (first + PAIR + 2) * ch, :]
        out = jnp.dot(
            w2_ref[...], jnp.concatenate([column(q), column(q + half)], axis=1), preferred_element_type=jnp.float32
        )
        for i in range(PAIR):
            for j in range(2):
                total = bias
                for tap in range(3):
                    first = (tap * PAIR + i) * ch
                    total = total + shifted(out[first : first + ch, j * z : (j + 1) * z], lane, tap, z)
                row = q + j * half + i + 1
                hidden_two[row * ch : (row + 1) * ch, :] = jnp.maximum(total, 0.0).astype(jnp.bfloat16)

    lane = lax.broadcasted_iota(jnp.int32, (2 * GROUP, z), 1)
    for g in range(0, groups, 2):
        column = lambda first: hidden_two[first * GROUP * ch : (first * GROUP + GROUP + 2) * ch, :]
        out = jnp.dot(
            w3_ref[...], jnp.concatenate([column(g), column(g + 1)], axis=1), preferred_element_type=jnp.float32
        )
        for j in range(2):
            total = None
            for tap in range(3):
                part = out[tap * 2 * GROUP : (tap + 1) * 2 * GROUP, j * z : (j + 1) * z]
                part = shifted(part, lane, tap, z)
                total = part if total is None else total + part
            first = (g + j) * GROUP
            for part in range(2):
                out_ref[0, part, first : first + GROUP, :] = (
                    padded[part, PAD + first : PAD + first + GROUP, :]
                    + total[part * GROUP : (part + 1) * GROUP]
                    + tail_ref[part * GROUP : (part + 1) * GROUP, :]
                )


def denoise(stride, field, normals, weights):
    _, _, x_size, z = field.shape
    w1, b1, w2, b2, w3, tail, step = weights
    ch = b1.shape[0]
    span = GROUP + 2 * PAD
    return pl.pallas_call(
        functools.partial(denoise_kernel, stride),
        in_specs=[VMEM] * 12,
        out_specs=VMEM,
        out_shape=jax.ShapeDtypeStruct(field.shape, jnp.float32),
        scratch_shapes=[
            pltpu.VMEM((2, x_size + 2 * PAD, z), jnp.float32),
            pltpu.VMEM((3, 2, x_size + 2 * PAD, z), jnp.bfloat16),
            pltpu.VMEM((6 * span, x_size // GROUP * z), jnp.bfloat16),
            pltpu.VMEM(((x_size + 2) * ch, z), jnp.bfloat16),
            pltpu.VMEM(((x_size + 2) * ch, z), jnp.bfloat16),
        ],
        cost_estimate=pl.CostEstimate(flops=4_000_000_000, bytes_accessed=2_000_000, transcendentals=0),
        compiler_params=pltpu.CompilerParams(vmem_limit_bytes=16 << 20),
        name="denoise",
    )(step, tail, field, *normals, w1, b1, w2, b2, w3)


def prepare_kernel(
    w_in_ref, b_in_ref, w_mid_ref, b_mid_ref, w_out_ref, b_out_ref, step_in_ref,
    w1_ref, b1_ref, w2_ref, b2_ref, w3_ref, tail_ref, step_ref,
):
    ch, z = b1_ref.shape
    span = GROUP + 2 * PAD
    step_ref[...] = jnp.full(step_ref.shape, step_in_ref[0])
    for part in range(2):
        tail_ref[part * GROUP : (part + 1) * GROUP, :] = jnp.full((GROUP, z), b_out_ref[part])
    b1_ref[...] = jnp.transpose(jnp.broadcast_to(b_in_ref[...], (z, ch)))
    b2_ref[...] = jnp.transpose(jnp.broadcast_to(b_mid_ref[...], (z, ch)))
    taps = w_in_ref[...]
    row = lax.broadcasted_iota(jnp.int32, (18, 6 * span), 0)
    column = lax.broadcasted_iota(jnp.int32, (18, 6 * span), 1)
    place = (row % 6) * span + row // 6 + (PAD - 1)
    for r in range(GROUP):
        select = jnp.where(column == place + r, 1.0, 0.0).astype(jnp.bfloat16)
        w1_ref[r * ch : (r + 1) * ch, :] = lax.dot_general(
            taps, select, (((0,), (0,)), ((), ())), preferred_element_type=jnp.float32
        ).astype(jnp.bfloat16)
    w2_ref[...] = jnp.zeros_like(w2_ref)
    for dz in range(3):
        for dx in range(3):
            block = w_mid_ref[dx, dz]
            for r in range(PAIR):
                first = (dz * PAIR + r) * ch
                w2_ref[first : first + ch, (r + dx) * ch : (r + dx + 1) * ch] = block
    wide = (GROUP, (GROUP + 2) * ch)
    offset = lax.broadcasted_iota(jnp.int32, wide, 1) // ch - lax.broadcasted_iota(jnp.int32, wide, 0)
    for dz in range(3):
        for part in range(2):
            total = jnp.zeros(wide, jnp.float32)
            for dx in range(3):
                line = w_out_ref[dx, dz, part : part + 1, :].astype(jnp.float32)
                line = jnp.concatenate([line] * (GROUP + 2), axis=1)
                total = jnp.where(offset == dx, jnp.broadcast_to(line, wide), total)
            first = (dz * 2 + part) * GROUP
            w3_ref[first : first + GROUP, :] = total.astype(jnp.bfloat16)


def prepare(w_in, b_in, w_mid, b_mid, w_out, b_out, step, x_size, z):
    ch = w_mid.shape[0]
    shapes = [
        jax.ShapeDtypeStruct((GROUP * ch, 6 * (GROUP + 2 * PAD)), jnp.bfloat16),
        jax.ShapeDtypeStruct((ch, z), jnp.float32),
        jax.ShapeDtypeStruct((3 * PAIR * ch, (PAIR + 2) * ch), jnp.bfloat16),
        jax.ShapeDtypeStruct((ch, z), jnp.float32),
        jax.ShapeDtypeStruct((6 * GROUP, (GROUP + 2) * ch), jnp.bfloat16),
        jax.ShapeDtypeStruct((2 * GROUP, z), jnp.float32),
        jax.ShapeDtypeStruct((x_size, z), jnp.float32),
    ]
    return pl.pallas_call(
        prepare_kernel,
        in_specs=[VMEM] * 5 + [SMEM] * 2,
        out_specs=[VMEM] * 7,
        out_shape=shapes,
        cost_estimate=pl.CostEstimate(flops=1_000_000_000, bytes_accessed=8_000_000, transcendentals=0),
        compiler_params=pltpu.CompilerParams(vmem_limit_bytes=8 << 20),
        name="prepare",
    )(
        w_in.transpose(2, 3, 1, 0).reshape(18, ch),
        b_in[None],
        w_mid.transpose(2, 3, 0, 1),
        b_mid[None],
        w_out.transpose(2, 3, 0, 1),
        b_out,
        step,
    )


def pack_kernel(stride, maps_ref, field_ref, one_ref, two_ref, three_ref, held, sems, field_sem):
    coils = maps_ref.shape[2]
    rows = one_ref.shape[2]
    share, distances = place(stride)
    field_copy = pltpu.make_async_copy(field_ref.at[0], held, field_sem)
    field_copy.start()
    copies = []
    outs = (one_ref, two_ref, three_ref)
    for i, ref in enumerate(outs):
        first = pl.multiple_of((share ^ distances[i]) * rows, rows)
        for part in range(2):
            copy = pltpu.make_async_copy(
                maps_ref.at[0, part, :, pl.ds(first, rows), :], ref.at[part, 0:coils], sems.at[i, part]
            )
            copy.start()
            copies.append(copy)
    field_copy.wait()
    for i, ref in enumerate(outs):
        first = pl.multiple_of((share ^ distances[i]) * rows, rows)
        for part in range(2):
            value = held[part, pl.ds(first, rows), :]
            high = value.astype(jnp.bfloat16)
            ref[part, coils] = high
            ref[part, coils + 1] = (value - high.astype(jnp.float32)).astype(jnp.bfloat16)
    for copy in copies:
        copy.wait()


def pack(stride, coil_maps, field):
    _, _, coils, x_size, z = coil_maps.shape
    piece = jax.ShapeDtypeStruct((2, coils + 2, x_size // FOLDS, z), jnp.bfloat16)
    return pl.pallas_call(
        functools.partial(pack_kernel, stride),
        in_specs=[HBM, HBM],
        out_specs=[VMEM] * 3,
        out_shape=[piece] * 3,
        scratch_shapes=[
            pltpu.VMEM((2, x_size, z), jnp.float32),
            pltpu.SemaphoreType.DMA((3, 2)),
            pltpu.SemaphoreType.DMA,
        ],
        cost_estimate=pl.CostEstimate(flops=0, bytes_accessed=2_000_000, transcendentals=0),
        compiler_params=pltpu.CompilerParams(vmem_limit_bytes=PACK_LIMIT),
        name="pack",
    )(*(pltpu.with_memory_space_constraint(array, pltpu.HBM) for array in (coil_maps, field)))


def per_device(zero_filled, coil_maps, offsets, step_sizes, w_in, b_in, w_mid, b_mid, w_out, b_out):
    devices = lax.axis_size("gy")
    stride = devices // FOLDS
    x_size, z = zero_filled.shape[2:]
    rows = x_size // FOLDS
    share = lax.axis_index("gy") // stride

    def trade(values):
        out = []
        for value, distances in zip(values, zip(*ORDERS)):
            pairs = [(j, (j // stride ^ distances[j % 2]) * stride + j % stride) for j in range(devices)]
            out.append(lax.ppermute(value, "gy", pairs))
        return out

    pieces = trade(pack(stride, coil_maps, zero_filled))
    weights = prepare(w_in, b_in, w_mid, b_mid, w_out, b_out, step_sizes, x_size, z)
    offs = lax.dynamic_slice_in_dim(offsets, share * rows, rows, 0)
    offs = jnp.broadcast_to(offs[:, None], (rows, z))
    pieces, weights, offs = lax.optimization_barrier((pieces, weights, offs))
    normals = fold(stride, coil_maps, zero_filled, pieces, offs)
    normals = [normals[0]] + trade(normals[1:])
    return denoise(stride, zero_filled, normals, weights)


def solution(mesh):
    in_specs = (
        P(("parts", "gy"), None, None, None),
        P(("parts", "gy"), None, None, None, None),
        P("parts"),
        P(),
        P(),
        P(),
        P(),
        P(),
        P(),
        P(),
    )
    out_specs = P(("parts", "gy"), None, None, None)
    return jax.shard_map(
        per_device, mesh=mesh, in_specs=in_specs, out_specs=out_specs, check_vma=False
    )
```

```python
import functools

import jax
import jax.numpy as jnp
from jax import lax
from jax.experimental import pallas as pl
from jax.experimental.pallas import tpu as pltpu
from jax.sharding import PartitionSpec as P

FOLDS = 4
GROUP = 16
QUAD = 4
PAIR = 2
PAD = 8
ORDERS = ((1, 2, 3), (3, 2, 1))
BACK = (3, 2, 1)
PACK_LIMIT = 8 << 20

VMEM = pl.BlockSpec(memory_space=pltpu.VMEM)
HBM = pl.BlockSpec(memory_space=pltpu.HBM)
SMEM = pl.BlockSpec(memory_space=pltpu.SMEM)


def place(stride):
    position = lax.axis_index("gy")
    odd = position % 2
    return position // stride, [jnp.where(odd == 0, even, other) for even, other in zip(*ORDERS)]


def fold_kernel(stride, maps_ref, field_ref, one_ref, two_ref, three_ref, offs_ref, out0, out1, out2, out3):
    coils = maps_ref.shape[2]
    rows = out0.shape[1]
    share, distances = place(stride)
    odd = distances[0] != ORDERS[0][0]
    own = pl.ds(pl.multiple_of(share * rows, rows), rows)
    offs = offs_ref[...]
    pieces = (None, one_ref, two_ref, three_ref)
    outs = (out0, out1, out2, out3)
    turned = []
    units = []
    for k in range(FOLDS):
        if k == 0:
            real, imag = field_ref[0, 0, own, :], field_ref[0, 1, own, :]
            turned.append((real, imag))
            units.append(None)
            continue
        piece = pieces[k]
        real = piece[0, coils].astype(jnp.float32) + piece[0, coils + 1].astype(jnp.float32)
        imag = piece[1, coils].astype(jnp.float32) + piece[1, coils + 1].astype(jnp.float32)
        turns = (((share ^ distances[k - 1]) - share) * offs) & 3
        zero, one = jnp.zeros_like(real), jnp.ones_like(real)
        cosine = jnp.where(turns == 0, one, jnp.where(turns == 2, -one, zero))
        sine = jnp.where(turns == 3, one, jnp.where(turns == 1, -one, zero))
        units.append((cosine, sine))
        turned.append((cosine * real - sine * imag, cosine * imag + sine * real))

    def step(c, sums):
        maps = []
        fold_real = fold_imag = None
        for k in range(FOLDS):
            if k == 0:
                real, imag = maps_ref[0, 0, c, own, :], maps_ref[0, 1, c, own, :]
            else:
                real, imag = pieces[k][0, c], pieces[k][1, c]
            real, imag = real.astype(jnp.float32), imag.astype(jnp.float32)
            maps.append((real, imag))
            term_real = real * turned[k][0] - imag * turned[k][1]
            term_imag = real * turned[k][1] + imag * turned[k][0]
            fold_real = term_real if k == 0 else fold_real + term_real
            fold_imag = term_imag if k == 0 else fold_imag + term_imag
        new = []
        for k in range(FOLDS):
            real, imag = maps[k]
            new.append(sums[2 * k] + (real * fold_real + imag * fold_imag))
            new.append(sums[2 * k + 1] + (real * fold_imag - imag * fold_real))
        return tuple(new)

    zeros = tuple(jnp.zeros(offs.shape, jnp.float32) for _ in range(2 * FOLDS))
    sums = lax.fori_loop(0, coils, step, zeros, unroll=8)
    out0[0], out0[1] = 0.25 * sums[0], 0.25 * sums[1]
    results = []
    for k in range(1, FOLDS):
        real, imag = 0.25 * sums[2 * k], 0.25 * sums[2 * k + 1]
        cosine, sine = units[k]
        results.append((cosine * real + sine * imag, cosine * imag - sine * real))
    for slot, distance in enumerate(BACK):
        even, other = (results[order.index(distance)] for order in ORDERS)
        for part in range(2):
            outs[slot + 1][part] = jnp.where(odd, other[part], even[part])


def fold(stride, coil_maps, field, pieces, offs):
    coils = coil_maps.shape[2]
    rows, z = offs.shape
    return pl.pallas_call(
        functools.partial(fold_kernel, stride),
        in_specs=[VMEM] * 6,
        out_specs=[VMEM] * FOLDS,
        out_shape=[jax.ShapeDtypeStruct((2, rows, z), jnp.float32)] * FOLDS,
        cost_estimate=pl.CostEstimate(flops=70 * coils * rows * z, bytes_accessed=16 * coils * rows * z, transcendentals=0),
        compiler_params=pltpu.CompilerParams(vmem_limit_bytes=8 << 20),
        name="fold",
    )(coil_maps, field, *pieces, offs)


def shifted(value, lane, tap, width):
    if tap == 1:
        return value
    if tap == 0:
        return jnp.where(lane == 0, 0.0, pltpu.roll(value, 1, 1))
    return jnp.where(lane == width - 1, 0.0, pltpu.roll(value, width - 1, 1))


def denoise_kernel(
    stride, step_ref, tail_ref, field_ref, own_ref, one_ref, two_ref, three_ref,
    w1_ref, b1_ref, w2_ref, b2_ref, w3_ref, out_ref, padded, window, low, hidden_one, hidden_two,
):
    _, _, x_size, z = field_ref.shape
    rows = own_ref.shape[1]
    ch = b1_ref.shape[0]
    share, _ = place(stride)
    groups = x_size // GROUP
    for k, ref in enumerate((own_ref, one_ref, two_ref, three_ref)):
        start = pl.multiple_of((share if k == 0 else share ^ BACK[k - 1]) * rows, rows)
        for part in range(2):
            padded[part, pl.ds(PAD + start, rows), :] = ref[part]
    edge = jnp.zeros((PAD, z), jnp.float32)
    for part in range(2):
        padded[part, 0:PAD, :] = edge
        padded[part, PAD + x_size : PAD + x_size + PAD, :] = edge
        base = field_ref[0, part]
        stepped = base - step_ref[...] * (padded[part, PAD : PAD + x_size, :] - base)
        padded[part, PAD : PAD + x_size, :] = stepped
    lane = lax.broadcasted_iota(jnp.int32, (x_size + 2 * PAD, z), 1)
    for tap in range(3):
        for part in range(2):
            window[tap, part] = shifted(padded[part], lane, tap, z).astype(jnp.bfloat16)
    span = GROUP + 2 * PAD
    for g in range(groups):
        for tap in range(3):
            for part in range(2):
                low[(tap * 2 + part) * span : (tap * 2 + part + 1) * span, g * z : (g + 1) * z] = window[
                    tap, part, g * GROUP : g * GROUP + span, :
                ]
    empty = jnp.zeros((ch, z), jnp.bfloat16)
    for hidden in (hidden_one, hidden_two):
        hidden[0:ch, :] = empty
        hidden[(x_size + 1) * ch : (x_size + 2) * ch, :] = empty

    bias = b1_ref[...]
    for r in range(0, GROUP, QUAD):
        for g in range(0, groups, 2):
            out = jnp.dot(
                w1_ref[r * ch : (r + QUAD) * ch, :], low[:, g * z : (g + 2) * z], preferred_element_type=jnp.float32
            )
            for i in range(QUAD):
                for j in range(2):
                    value = jnp.maximum(out[i * ch : (i + 1) * ch, j * z : (j + 1) * z] + bias, 0.0)
                    row = (g + j) * GROUP + r + i + 1
                    hidden_one[row * ch : (row + 1) * ch, :] = value.astype(jnp.bfloat16)

    bias = b2_ref[...]
    lane = lax.broadcasted_iota(jnp.int32, (ch, z), 1)
    half = x_size // 2
    for q in range(0, half, PAIR):
        column = lambda first: hidden_one[first * ch : (first + PAIR + 2) * ch, :]
        out = jnp.dot(
            w2_ref[...], jnp.concatenate([column(q), column(q + half)], axis=1), preferred_element_type=jnp.float32
        )
        for i in range(PAIR):
            for j in range(2):
                total = bias
                for tap in range(3):
                    first = (tap * PAIR + i) * ch
                    total = total + shifted(out[first : first + ch, j * z : (j + 1) * z], lane, tap, z)
                row = q + j * half + i + 1
                hidden_two[row * ch : (row + 1) * ch, :] = jnp.maximum(total, 0.0).astype(jnp.bfloat16)

    lane = lax.broadcasted_iota(jnp.int32, (2 * GROUP, z), 1)
    for g in range(0, groups, 2):
        column = lambda first: hidden_two[first * GROUP * ch : (first * GROUP + GROUP + 2) * ch, :]
        out = jnp.dot(
            w3_ref[...], jnp.concatenate([column(g), column(g + 1)], axis=1), preferred_element_type=jnp.float32
        )
        for j in range(2):
            total = None
            for tap in range(3):
                part = out[tap * 2 * GROUP : (tap + 1) * 2 * GROUP, j * z : (j + 1) * z]
                part = shifted(part, lane, tap, z)
                total = part if total is None else total + part
            first = (g + j) * GROUP
            for part in range(2):
                out_ref[0, part, first : first + GROUP, :] = (
                    padded[part, PAD + first : PAD + first + GROUP, :]
                    + total[part * GROUP : (part + 1) * GROUP]
                    + tail_ref[part * GROUP : (part + 1) * GROUP, :]
                )


def denoise(stride, field, normals, weights):
    _, _, x_size, z = field.shape
    w1, b1, w2, b2, w3, tail, step = weights
    ch = b1.shape[0]
    span = GROUP + 2 * PAD
    return pl.pallas_call(
        functools.partial(denoise_kernel, stride),
        in_specs=[VMEM] * 12,
        out_specs=VMEM,
        out_shape=jax.ShapeDtypeStruct(field.shape, jnp.float32),
        scratch_shapes=[
            pltpu.VMEM((2, x_size + 2 * PAD, z), jnp.float32),
            pltpu.VMEM((3, 2, x_size + 2 * PAD, z), jnp.bfloat16),
            pltpu.VMEM((6 * span, x_size // GROUP * z), jnp.bfloat16),
            pltpu.VMEM(((x_size + 2) * ch, z), jnp.bfloat16),
            pltpu.VMEM(((x_size + 2) * ch, z), jnp.bfloat16),
        ],
        cost_estimate=pl.CostEstimate(flops=4_000_000_000, bytes_accessed=2_000_000, transcendentals=0),
        compiler_params=pltpu.CompilerParams(vmem_limit_bytes=16 << 20),
        name="denoise",
    )(step, tail, field, *normals, w1, b1, w2, b2, w3)


def prepare_kernel(
    w_in_ref, b_in_ref, w_mid_ref, b_mid_ref, w_out_ref, b_out_ref, step_in_ref,
    w1_ref, b1_ref, w2_ref, b2_ref, w3_ref, tail_ref, step_ref,
):
    ch, z = b1_ref.shape
    span = GROUP + 2 * PAD
    step_ref[...] = jnp.full(step_ref.shape, step_in_ref[0])
    for part in range(2):
        tail_ref[part * GROUP : (part + 1) * GROUP, :] = jnp.full((GROUP, z), b_out_ref[part])
    b1_ref[...] = jnp.transpose(jnp.broadcast_to(b_in_ref[...], (z, ch)))
    b2_ref[...] = jnp.transpose(jnp.broadcast_to(b_mid_ref[...], (z, ch)))
    taps = w_in_ref[...]
    row = lax.broadcasted_iota(jnp.int32, (18, 6 * span), 0)
    column = lax.broadcasted_iota(jnp.int32, (18, 6 * span), 1)
    place = (row % 6) * span + row // 6 + (PAD - 1)
    for r in range(GROUP):
        select = jnp.where(column == place + r, 1.0, 0.0).astype(jnp.bfloat16)
        w1_ref[r * ch : (r + 1) * ch, :] = lax.dot_general(
            taps, select, (((0,), (0,)), ((), ())), preferred_element_type=jnp.float32
        ).astype(jnp.bfloat16)
    w2_ref[...] = jnp.zeros_like(w2_ref)
    for dz in range(3):
        for dx in range(3):
            block = w_mid_ref[dx, dz]
            for r in range(PAIR):
                first = (dz * PAIR + r) * ch
                w2_ref[first : first + ch, (r + dx) * ch : (r + dx + 1) * ch] = block
    wide = (GROUP, (GROUP + 2) * ch)
    offset = lax.broadcasted_iota(jnp.int32, wide, 1) // ch - lax.broadcasted_iota(jnp.int32, wide, 0)
    for dz in range(3):
        for part in range(2):
            total = jnp.zeros(wide, jnp.float32)
            for dx in range(3):
                line = w_out_ref[dx, dz, part : part + 1, :].astype(jnp.float32)
                line = jnp.concatenate([line] * (GROUP + 2), axis=1)
                total = jnp.where(offset == dx, jnp.broadcast_to(line, wide), total)
            first = (dz * 2 + part) * GROUP
            w3_ref[first : first + GROUP, :] = total.astype(jnp.bfloat16)


def prepare(w_in, b_in, w_mid, b_mid, w_out, b_out, step, x_size, z):
    ch = w_mid.shape[0]
    shapes = [
        jax.ShapeDtypeStruct((GROUP * ch, 6 * (GROUP + 2 * PAD)), jnp.bfloat16),
        jax.ShapeDtypeStruct((ch, z), jnp.float32),
        jax.ShapeDtypeStruct((3 * PAIR * ch, (PAIR + 2) * ch), jnp.bfloat16),
        jax.ShapeDtypeStruct((ch, z), jnp.float32),
        jax.ShapeDtypeStruct((6 * GROUP, (GROUP + 2) * ch), jnp.bfloat16),
        jax.ShapeDtypeStruct((2 * GROUP, z), jnp.float32),
        jax.ShapeDtypeStruct((x_size, z), jnp.float32),
    ]
    return pl.pallas_call(
        prepare_kernel,
        in_specs=[VMEM] * 5 + [SMEM] * 2,
        out_specs=[VMEM] * 7,
        out_shape=shapes,
        cost_estimate=pl.CostEstimate(flops=1_000_000_000, bytes_accessed=8_000_000, transcendentals=0),
        compiler_params=pltpu.CompilerParams(vmem_limit_bytes=8 << 20),
        name="prepare",
    )(
        w_in.transpose(2, 3, 1, 0).reshape(18, ch),
        b_in[None],
        w_mid.transpose(2, 3, 0, 1),
        b_mid[None],
        w_out.transpose(2, 3, 0, 1),
        b_out,
        step,
    )


def pack_kernel(stride, maps_ref, field_ref, one_ref, two_ref, three_ref, held, sems, field_sem):
    coils = maps_ref.shape[2]
    rows = one_ref.shape[2]
    share, distances = place(stride)
    field_copy = pltpu.make_async_copy(field_ref.at[0], held, field_sem)
    field_copy.start()
    copies = []
    outs = (one_ref, two_ref, three_ref)
    for i, ref in enumerate(outs):
        first = pl.multiple_of((share ^ distances[i]) * rows, rows)
        for part in range(2):
            copy = pltpu.make_async_copy(
                maps_ref.at[0, part, :, pl.ds(first, rows), :], ref.at[part, 0:coils], sems.at[i, part]
            )
            copy.start()
            copies.append(copy)
    field_copy.wait()
    for i, ref in enumerate(outs):
        first = pl.multiple_of((share ^ distances[i]) * rows, rows)
        for part in range(2):
            value = held[part, pl.ds(first, rows), :]
            high = value.astype(jnp.bfloat16)
            ref[part, coils] = high
            ref[part, coils + 1] = (value - high.astype(jnp.float32)).astype(jnp.bfloat16)
    for copy in copies:
        copy.wait()


def pack(stride, coil_maps, field):
    _, _, coils, x_size, z = coil_maps.shape
    piece = jax.ShapeDtypeStruct((2, coils + 2, x_size // FOLDS, z), jnp.bfloat16)
    return pl.pallas_call(
        functools.partial(pack_kernel, stride),
        in_specs=[HBM, HBM],
        out_specs=[VMEM] * 3,
        out_shape=[piece] * 3,
        scratch_shapes=[
            pltpu.VMEM((2, x_size, z), jnp.float32),
            pltpu.SemaphoreType.DMA((3, 2)),
            pltpu.SemaphoreType.DMA,
        ],
        cost_estimate=pl.CostEstimate(flops=0, bytes_accessed=2_000_000, transcendentals=0),
        compiler_params=pltpu.CompilerParams(vmem_limit_bytes=PACK_LIMIT),
        name="pack",
    )(*(pltpu.with_memory_space_constraint(array, pltpu.HBM) for array in (coil_maps, field)))


def per_device(zero_filled, coil_maps, offsets, step_sizes, w_in, b_in, w_mid, b_mid, w_out, b_out):
    devices = lax.axis_size("gy")
    stride = devices // FOLDS
    x_size, z = zero_filled.shape[2:]
    rows = x_size // FOLDS
    share = lax.axis_index("gy") // stride

    def trade(values, *orders):
        out = []
        for value, distances in zip(values, zip(*orders)):
            pairs = [(j, (j // stride ^ distances[j % 2]) * stride + j % stride) for j in range(devices)]
            out.append(lax.ppermute(value, "gy", pairs))
        return out

    pieces = trade(pack(stride, coil_maps, zero_filled), *ORDERS)
    weights = prepare(w_in, b_in, w_mid, b_mid, w_out, b_out, step_sizes, x_size, z)
    offs = lax.dynamic_slice_in_dim(offsets, share * rows, rows, 0)
    offs = jnp.broadcast_to(offs[:, None], (rows, z))
    pieces, weights, offs = lax.optimization_barrier((pieces, weights, offs))
    normals = fold(stride, coil_maps, zero_filled, pieces, offs)
    normals = [normals[0]] + trade(normals[1:], BACK, BACK)
    return denoise(stride, zero_filled, normals, weights)


def solution(mesh):
    in_specs = (
        P(("parts", "gy"), None, None, None),
        P(("parts", "gy"), None, None, None, None),
        P("parts"),
        P(),
        P(),
        P(),
        P(),
        P(),
        P(),
        P(),
    )
    out_specs = P(("parts", "gy"), None, None, None)
    return jax.shard_map(
        per_device, mesh=mesh, in_specs=in_specs, out_specs=out_specs, check_vma=False
    )
```

```python
import functools

import jax
import jax.numpy as jnp
from jax import lax
from jax.experimental import pallas as pl
from jax.experimental.pallas import tpu as pltpu
from jax.sharding import PartitionSpec as P

FOLDS = 4
GROUP = 16
QUAD = 4
PAIR = 2
PAD = 8
ORDERS = ((1, 2, 3), (3, 2, 1))
BACK = (3, 2, 1)
PACK_LIMIT = 8 << 20
CHUNKS = 2
SENT = ((0, (0, 1)), (1, (0,)), (2, (0,)), (1, (1,)), (2, (1,)))

VMEM = pl.BlockSpec(memory_space=pltpu.VMEM)
HBM = pl.BlockSpec(memory_space=pltpu.HBM)
SMEM = pl.BlockSpec(memory_space=pltpu.SMEM)


def place(stride):
    position = lax.axis_index("gy")
    odd = position % 2
    return position // stride, [jnp.where(odd == 0, even, other) for even, other in zip(*ORDERS)]


def fold_kernel(stride, chunk, maps_ref, field_ref, one_ref, two_ref, three_ref, offs_ref, out0, out1, out2, out3):
    coils = maps_ref.shape[2]
    rows = out0.shape[1]
    share, distances = place(stride)
    odd = distances[0] != ORDERS[0][0]
    own = pl.ds(pl.multiple_of((chunk * FOLDS + share) * rows, rows), rows)
    offs = offs_ref[chunk]
    pieces = (None, one_ref.at[:, :, pl.ds(chunk * rows, rows), :], two_ref, three_ref)
    outs = (out0, out1, out2, out3)
    turned = []
    units = []
    for k in range(FOLDS):
        if k == 0:
            real, imag = field_ref[0, 0, own, :], field_ref[0, 1, own, :]
            turned.append((real, imag))
            units.append(None)
            continue
        piece = pieces[k]
        real = piece[0, coils].astype(jnp.float32) + piece[0, coils + 1].astype(jnp.float32)
        imag = piece[1, coils].astype(jnp.float32) + piece[1, coils + 1].astype(jnp.float32)
        turns = (((share ^ distances[k - 1]) - share) * offs) & 3
        zero, one = jnp.zeros_like(real), jnp.ones_like(real)
        cosine = jnp.where(turns == 0, one, jnp.where(turns == 2, -one, zero))
        sine = jnp.where(turns == 3, one, jnp.where(turns == 1, -one, zero))
        units.append((cosine, sine))
        turned.append((cosine * real - sine * imag, cosine * imag + sine * real))

    def step(c, sums):
        maps = []
        fold_real = fold_imag = None
        for k in range(FOLDS):
            if k == 0:
                real, imag = maps_ref[0, 0, c, own, :], maps_ref[0, 1, c, own, :]
            else:
                real, imag = pieces[k][0, c], pieces[k][1, c]
            real, imag = real.astype(jnp.float32), imag.astype(jnp.float32)
            maps.append((real, imag))
            term_real = real * turned[k][0] - imag * turned[k][1]
            term_imag = real * turned[k][1] + imag * turned[k][0]
            fold_real = term_real if k == 0 else fold_real + term_real
            fold_imag = term_imag if k == 0 else fold_imag + term_imag
        new = []
        for k in range(FOLDS):
            real, imag = maps[k]
            new.append(sums[2 * k] + (real * fold_real + imag * fold_imag))
            new.append(sums[2 * k + 1] + (real * fold_imag - imag * fold_real))
        return tuple(new)

    zeros = tuple(jnp.zeros(offs.shape, jnp.float32) for _ in range(2 * FOLDS))
    sums = lax.fori_loop(0, coils, step, zeros, unroll=8)
    out0[0], out0[1] = 0.25 * sums[0], 0.25 * sums[1]
    results = []
    for k in range(1, FOLDS):
        real, imag = 0.25 * sums[2 * k], 0.25 * sums[2 * k + 1]
        cosine, sine = units[k]
        results.append((cosine * real + sine * imag, cosine * imag - sine * real))
    for slot, distance in enumerate(BACK):
        even, other = (results[order.index(distance)] for order in ORDERS)
        for part in range(2):
            outs[slot + 1][part] = jnp.where(odd, other[part], even[part])


def fold(stride, chunk, coil_maps, field, pieces, offs):
    coils = coil_maps.shape[2]
    _, rows, z = offs.shape
    return pl.pallas_call(
        functools.partial(fold_kernel, stride, chunk),
        in_specs=[VMEM] * 6,
        out_specs=[VMEM] * FOLDS,
        out_shape=[jax.ShapeDtypeStruct((2, rows, z), jnp.float32)] * FOLDS,
        cost_estimate=pl.CostEstimate(flops=70 * coils * rows * z, bytes_accessed=16 * coils * rows * z, transcendentals=0),
        compiler_params=pltpu.CompilerParams(vmem_limit_bytes=8 << 20),
        name="fold",
    )(coil_maps, field, *pieces, offs)


def shifted(value, lane, tap, width):
    if tap == 1:
        return value
    if tap == 0:
        return jnp.where(lane == 0, 0.0, pltpu.roll(value, 1, 1))
    return jnp.where(lane == width - 1, 0.0, pltpu.roll(value, width - 1, 1))


def denoise_kernel(stride, chunk, *refs):
    step_ref, tail_ref, field_ref, w1_ref, b1_ref, w2_ref, b2_ref, w3_ref, *normals = refs[:12]
    padded, window, low, hidden_one, hidden_two = refs[-5:]
    _, _, x_size, z = field_ref.shape
    ch = b1_ref.shape[0]
    half = x_size // 2
    cut = half - QUAD
    if chunk == 0:
        out_ref, line_ref, one_ref, two_ref = refs[12:16]
        begin, end, blank = 0, half, 0
    else:
        done_ref, line_ref, one_ref, two_ref, out_ref = refs[12:17]
        begin, end, blank = half, x_size, half - GROUP
    share, _ = place(stride)
    rows = normals[0].shape[1]
    for k, ref in enumerate(normals):
        source = share if k == 0 else share ^ BACK[k - 1]
        start = pl.multiple_of(PAD + begin + source * rows, rows)
        for part in range(2):
            padded[part, pl.ds(start, rows), :] = ref[part]
    edge = jnp.zeros((PAD, z), jnp.float32)
    for part in range(2):
        padded[part, PAD + end : PAD + end + PAD, :] = edge
        if chunk == 0:
            padded[part, 0:PAD, :] = edge
        else:
            padded[part, half - GROUP : half - GROUP + PAD, :] = edge
            padded[part, half - GROUP + PAD : half - GROUP + 2 * PAD, :] = edge
            padded[part, half : half + PAD, :] = line_ref[part]
        base = field_ref[0, part, begin:end, :]
        stepped = base - step_ref[begin:end, :] * (padded[part, PAD + begin : PAD + end, :] - base)
        padded[part, PAD + begin : PAD + end, :] = stepped
    first, last = blank, end + 2 * PAD
    lane = lax.broadcasted_iota(jnp.int32, (last - first, z), 1)
    for tap in range(3):
        for part in range(2):
            window[tap, part, first:last, :] = shifted(padded[part, first:last, :], lane, tap, z).astype(jnp.bfloat16)
    span = GROUP + 2 * PAD
    groups = range(blank // GROUP, end // GROUP)
    for g in groups:
        for tap in range(3):
            for part in range(2):
                low[(tap * 2 + part) * span : (tap * 2 + part + 1) * span, g * z : (g + 1) * z] = window[
                    tap, part, g * GROUP : g * GROUP + span, :
                ]

    def block(x, count=1):
        return slice((x + 1) * ch, (x + 1 + count) * ch)

    empty = jnp.zeros((ch, z), jnp.bfloat16)
    hidden_one[block(end)] = empty
    hidden_two[block(end)] = empty
    if chunk == 0:
        hidden_one[block(-1)] = empty
        hidden_two[block(-1)] = empty
    else:
        hidden_one[block(cut - 1, QUAD)] = one_ref[...]
        for x in range(half - GROUP - 1, cut - 1):
            hidden_two[block(x)] = empty
        hidden_two[block(cut - 1)] = two_ref[...]

    bias = b1_ref[...]
    if chunk == 1:
        g = half // GROUP - 1
        out = jnp.dot(
            w1_ref[(GROUP - 1) * ch :, :], low[:, g * z : (g + 1) * z], preferred_element_type=jnp.float32
        )
        hidden_one[block(half - 1)] = jnp.maximum(out + bias, 0.0).astype(jnp.bfloat16)
    for r in range(0, GROUP, QUAD):
        for g in range(begin // GROUP, end // GROUP, 2):
            out = jnp.dot(
                w1_ref[r * ch : (r + QUAD) * ch, :], low[:, g * z : (g + 2) * z], preferred_element_type=jnp.float32
            )
            for i in range(QUAD):
                for j in range(2):
                    value = jnp.maximum(out[i * ch : (i + 1) * ch, j * z : (j + 1) * z] + bias, 0.0)
                    hidden_one[block((g + j) * GROUP + r + i)] = value.astype(jnp.bfloat16)

    bias = b2_ref[...]
    lane = lax.broadcasted_iota(jnp.int32, (ch, z), 1)
    start = 0 if chunk == 0 else cut
    stride = (end - start) // 2
    for q in range(start, start + stride, PAIR):
        out = jnp.dot(
            w2_ref[...],
            jnp.concatenate([hidden_one[block(q - 1, PAIR + 2)], hidden_one[block(q + stride - 1, PAIR + 2)]], axis=1),
            preferred_element_type=jnp.float32,
        )
        for i in range(PAIR):
            for j in range(2):
                total = bias
                for tap in range(3):
                    at = (tap * PAIR + i) * ch
                    total = total + shifted(out[at : at + ch, j * z : (j + 1) * z], lane, tap, z)
                hidden_two[block(q + j * stride + i)] = jnp.maximum(total, 0.0).astype(jnp.bfloat16)

    lane = lax.broadcasted_iota(jnp.int32, (2 * GROUP, z), 1)
    starts = [g * GROUP for g in groups]
    out = jnp.dot(
        w3_ref[...],
        jnp.concatenate([hidden_two[block(x - 1, GROUP + 2)] for x in starts], axis=1),
        preferred_element_type=jnp.float32,
    )
    for j, x in enumerate(starts):
        total = None
        for tap in range(3):
            part = out[tap * 2 * GROUP : (tap + 1) * 2 * GROUP, j * z : (j + 1) * z]
            part = shifted(part, lane, tap, z)
            total = part if total is None else total + part
        for part in range(2):
            value = (
                padded[part, PAD + x : PAD + x + GROUP, :]
                + total[part * GROUP : (part + 1) * GROUP]
                + tail_ref[part * GROUP : (part + 1) * GROUP, :]
            )
            if chunk == 0:
                out_ref[part, x : x + GROUP, :] = value
            elif x < half:
                keep = lax.broadcasted_iota(jnp.int32, (GROUP, z), 0) < cut - x
                out_ref[0, part, 0:x, :] = done_ref[part, 0:x, :]
                out_ref[0, part, x:half, :] = jnp.where(keep, done_ref[part, x:half, :], value)
            else:
                out_ref[0, part, x : x + GROUP, :] = value
    if chunk == 0:
        for part in range(2):
            line_ref[part] = padded[part, half : half + PAD, :]
        one_ref[...] = hidden_one[block(cut - 1, QUAD)]
        two_ref[...] = hidden_two[block(cut - 1)]


def denoise(stride, chunk, field, normals, weights, state):
    _, _, x_size, z = field.shape
    w1, b1, w2, b2, w3, tail, step = weights
    ch = b1.shape[0]
    span = GROUP + 2 * PAD
    if chunk == 0:
        out_shape = [
            jax.ShapeDtypeStruct((2, x_size // 2, z), jnp.float32),
            jax.ShapeDtypeStruct((2, PAD, z), jnp.float32),
            jax.ShapeDtypeStruct((QUAD * ch, z), jnp.bfloat16),
            jax.ShapeDtypeStruct((ch, z), jnp.bfloat16),
        ]
        out_specs = [VMEM] * 4
    else:
        out_shape = jax.ShapeDtypeStruct(field.shape, jnp.float32)
        out_specs = VMEM
    return pl.pallas_call(
        functools.partial(denoise_kernel, stride, chunk),
        in_specs=[VMEM] * (12 + len(state)),
        out_specs=out_specs,
        out_shape=out_shape,
        scratch_shapes=[
            pltpu.VMEM((2, x_size + 2 * PAD, z), jnp.float32),
            pltpu.VMEM((3, 2, x_size + 2 * PAD, z), jnp.bfloat16),
            pltpu.VMEM((6 * span, x_size // GROUP * z), jnp.bfloat16),
            pltpu.VMEM(((x_size + 2) * ch, z), jnp.bfloat16),
            pltpu.VMEM(((x_size + 2) * ch, z), jnp.bfloat16),
        ],
        cost_estimate=pl.CostEstimate(flops=2_000_000_000, bytes_accessed=2_000_000, transcendentals=0),
        compiler_params=pltpu.CompilerParams(vmem_limit_bytes=16 << 20),
        name=("denoise_first", "denoise_rest")[chunk],
    )(step, tail, field, w1, b1, w2, b2, w3, *normals, *state)


def prepare_kernel(
    w_in_ref, b_in_ref, w_mid_ref, b_mid_ref, w_out_ref, b_out_ref, step_in_ref,
    w1_ref, b1_ref, w2_ref, b2_ref, w3_ref, tail_ref, step_ref,
):
    ch, z = b1_ref.shape
    span = GROUP + 2 * PAD
    step_ref[...] = jnp.full(step_ref.shape, step_in_ref[0])
    for part in range(2):
        tail_ref[part * GROUP : (part + 1) * GROUP, :] = jnp.full((GROUP, z), b_out_ref[part])
    b1_ref[...] = jnp.transpose(jnp.broadcast_to(b_in_ref[...], (z, ch)))
    b2_ref[...] = jnp.transpose(jnp.broadcast_to(b_mid_ref[...], (z, ch)))
    taps = w_in_ref[...]
    row = lax.broadcasted_iota(jnp.int32, (18, 6 * span), 0)
    column = lax.broadcasted_iota(jnp.int32, (18, 6 * span), 1)
    place = (row % 6) * span + row // 6 + (PAD - 1)
    for r in range(GROUP):
        select = jnp.where(column == place + r, 1.0, 0.0).astype(jnp.bfloat16)
        w1_ref[r * ch : (r + 1) * ch, :] = lax.dot_general(
            taps, select, (((0,), (0,)), ((), ())), preferred_element_type=jnp.float32
        ).astype(jnp.bfloat16)
    w2_ref[...] = jnp.zeros_like(w2_ref)
    for dz in range(3):
        for dx in range(3):
            block = w_mid_ref[dx, dz]
            for r in range(PAIR):
                first = (dz * PAIR + r) * ch
                w2_ref[first : first + ch, (r + dx) * ch : (r + dx + 1) * ch] = block
    wide = (GROUP, (GROUP + 2) * ch)
    offset = lax.broadcasted_iota(jnp.int32, wide, 1) // ch - lax.broadcasted_iota(jnp.int32, wide, 0)
    for dz in range(3):
        for part in range(2):
            total = jnp.zeros(wide, jnp.float32)
            for dx in range(3):
                line = w_out_ref[dx, dz, part : part + 1, :].astype(jnp.float32)
                line = jnp.concatenate([line] * (GROUP + 2), axis=1)
                total = jnp.where(offset == dx, jnp.broadcast_to(line, wide), total)
            first = (dz * 2 + part) * GROUP
            w3_ref[first : first + GROUP, :] = total.astype(jnp.bfloat16)


def prepare(w_in, b_in, w_mid, b_mid, w_out, b_out, step, x_size, z):
    ch = w_mid.shape[0]
    shapes = [
        jax.ShapeDtypeStruct((GROUP * ch, 6 * (GROUP + 2 * PAD)), jnp.bfloat16),
        jax.ShapeDtypeStruct((ch, z), jnp.float32),
        jax.ShapeDtypeStruct((3 * PAIR * ch, (PAIR + 2) * ch), jnp.bfloat16),
        jax.ShapeDtypeStruct((ch, z), jnp.float32),
        jax.ShapeDtypeStruct((6 * GROUP, (GROUP + 2) * ch), jnp.bfloat16),
        jax.ShapeDtypeStruct((2 * GROUP, z), jnp.float32),
        jax.ShapeDtypeStruct((x_size, z), jnp.float32),
    ]
    return pl.pallas_call(
        prepare_kernel,
        in_specs=[VMEM] * 5 + [SMEM] * 2,
        out_specs=[VMEM] * 7,
        out_shape=shapes,
        cost_estimate=pl.CostEstimate(flops=1_000_000_000, bytes_accessed=8_000_000, transcendentals=0),
        compiler_params=pltpu.CompilerParams(vmem_limit_bytes=8 << 20),
        name="prepare",
    )(
        w_in.transpose(2, 3, 1, 0).reshape(18, ch),
        b_in[None],
        w_mid.transpose(2, 3, 0, 1),
        b_mid[None],
        w_out.transpose(2, 3, 0, 1),
        b_out,
        step,
    )


def pack_kernel(stride, maps_ref, field_ref, *refs):
    outs, (held, sems, field_sem) = refs[:-3], refs[-3:]
    coils = maps_ref.shape[2]
    rows = outs[-1].shape[2]
    share, distances = place(stride)
    field_copy = pltpu.make_async_copy(field_ref.at[0], held, field_sem)
    field_copy.start()
    copies = []
    spans = []
    for ref, (i, chunks) in zip(outs, SENT):
        for at, chunk in enumerate(chunks):
            first = pl.multiple_of((chunk * FOLDS + (share ^ distances[i])) * rows, rows)
            here, there = pl.ds(first, rows), pl.ds(at * rows, rows)
            spans.append((ref, here, there))
            for part in range(2):
                copy = pltpu.make_async_copy(
                    maps_ref.at[0, part, :, here, :], ref.at[part, 0:coils, there, :], sems.at[len(copies)]
                )
                copy.start()
                copies.append(copy)
    field_copy.wait()
    for ref, here, there in spans:
        for part in range(2):
            value = held[part, here, :]
            high = value.astype(jnp.bfloat16)
            ref[part, coils, there, :] = high
            ref[part, coils + 1, there, :] = (value - high.astype(jnp.float32)).astype(jnp.bfloat16)
    for copy in copies:
        copy.wait()


def pack(stride, coil_maps, field):
    _, _, coils, x_size, z = coil_maps.shape
    rows = x_size // FOLDS // CHUNKS
    pieces = [jax.ShapeDtypeStruct((2, coils + 2, len(chunks) * rows, z), jnp.bfloat16) for _, chunks in SENT]
    return pl.pallas_call(
        functools.partial(pack_kernel, stride),
        in_specs=[HBM, HBM],
        out_specs=[VMEM] * len(pieces),
        out_shape=pieces,
        scratch_shapes=[
            pltpu.VMEM((2, x_size, z), jnp.float32),
            pltpu.SemaphoreType.DMA((2 * sum(len(chunks) for _, chunks in SENT),)),
            pltpu.SemaphoreType.DMA,
        ],
        cost_estimate=pl.CostEstimate(flops=0, bytes_accessed=2_000_000, transcendentals=0),
        compiler_params=pltpu.CompilerParams(vmem_limit_bytes=PACK_LIMIT),
        name="pack",
    )(*(pltpu.with_memory_space_constraint(array, pltpu.HBM) for array in (coil_maps, field)))


def per_device(zero_filled, coil_maps, offsets, step_sizes, w_in, b_in, w_mid, b_mid, w_out, b_out):
    devices = lax.axis_size("gy")
    stride = devices // FOLDS
    x_size, z = zero_filled.shape[2:]
    rows = x_size // FOLDS // CHUNKS
    share = lax.axis_index("gy") // stride

    def trade(value, distances):
        pairs = [(j, (j // stride ^ distances[j % 2]) * stride + j % stride) for j in range(devices)]
        return lax.ppermute(value, "gy", pairs)

    sent = pack(stride, coil_maps, zero_filled)
    pieces = [trade(value, [order[i] for order in ORDERS]) for value, (i, _) in zip(sent, SENT)]
    chunks = [
        [next(piece for piece, (j, held) in zip(pieces, SENT) if i == j and chunk in held) for i in range(FOLDS - 1)]
        for chunk in range(CHUNKS)
    ]
    weights = prepare(w_in, b_in, w_mid, b_mid, w_out, b_out, step_sizes, x_size, z)
    offs = lax.dynamic_index_in_dim(offsets.reshape(CHUNKS, FOLDS, rows), share, 1, keepdims=False)
    offs = jnp.broadcast_to(offs[:, :, None], (CHUNKS, rows, z))
    chunks[0], weights, offs = lax.optimization_barrier((chunks[0], weights, offs))
    first = fold(stride, 0, coil_maps, zero_filled, chunks[0], offs)
    first = [first[0]] + [trade(value, (k, k)) for value, k in zip(first[1:], BACK)]
    rest = fold(stride, 1, coil_maps, zero_filled, chunks[1], offs)
    back = [trade(value, (k, k)) for value, k in zip(rest[1:], BACK)]
    first, own = lax.optimization_barrier((first, rest[0]))
    state = denoise(stride, 0, zero_filled, first, weights, [])
    return denoise(stride, 1, zero_filled, [own] + back, weights, state)


def solution(mesh):
    in_specs = (
        P(("parts", "gy"), None, None, None),
        P(("parts", "gy"), None, None, None, None),
        P("parts"),
        P(),
        P(),
        P(),
        P(),
        P(),
        P(),
        P(),
    )
    out_specs = P(("parts", "gy"), None, None, None)
    return jax.shard_map(
        per_device, mesh=mesh, in_specs=in_specs, out_specs=out_specs, check_vma=False
    )
```

```python
import functools

import jax
import jax.numpy as jnp
from jax import lax
from jax.experimental import pallas as pl
from jax.experimental.pallas import tpu as pltpu
from jax.sharding import PartitionSpec as P

FOLDS = 4
GROUP = 16
QUAD = 4
PAIR = 2
PAD = 8
ORDERS = ((1, 2, 3), (3, 2, 1))
BACK = (3, 2, 1)
PACK_LIMIT = 8 << 20
CHUNKS = 2
SENT = ((0, (0, 1)), (1, (0,)), (2, (0,)), (1, (1,)), (2, (1,)))

VMEM = pl.BlockSpec(memory_space=pltpu.VMEM)
HBM = pl.BlockSpec(memory_space=pltpu.HBM)
SMEM = pl.BlockSpec(memory_space=pltpu.SMEM)


def place(stride):
    position = lax.axis_index("gy")
    odd = position % 2
    return position // stride, [jnp.where(odd == 0, even, other) for even, other in zip(*ORDERS)]


def fold_kernel(stride, chunk, maps_ref, field_ref, one_ref, two_ref, three_ref, offs_ref, out0, out1, out2, out3):
    coils = maps_ref.shape[2]
    rows = out0.shape[1]
    share, distances = place(stride)
    odd = distances[0] != ORDERS[0][0]
    own = pl.ds(pl.multiple_of((chunk * FOLDS + share) * rows, rows), rows)
    offs = offs_ref[chunk]
    pieces = (None, one_ref.at[:, :, pl.ds(chunk * rows, rows), :], two_ref, three_ref)
    outs = (out0, out1, out2, out3)
    turned = []
    units = []
    for k in range(FOLDS):
        if k == 0:
            real, imag = field_ref[0, 0, own, :], field_ref[0, 1, own, :]
            turned.append((real, imag))
            units.append(None)
            continue
        piece = pieces[k]
        real = piece[0, coils].astype(jnp.float32) + piece[0, coils + 1].astype(jnp.float32)
        imag = piece[1, coils].astype(jnp.float32) + piece[1, coils + 1].astype(jnp.float32)
        turns = (((share ^ distances[k - 1]) - share) * offs) & 3
        zero, one = jnp.zeros_like(real), jnp.ones_like(real)
        cosine = jnp.where(turns == 0, one, jnp.where(turns == 2, -one, zero))
        sine = jnp.where(turns == 3, one, jnp.where(turns == 1, -one, zero))
        units.append((cosine, sine))
        turned.append((cosine * real - sine * imag, cosine * imag + sine * real))

    def step(c, sums):
        maps = []
        fold_real = fold_imag = None
        for k in range(FOLDS):
            if k == 0:
                real, imag = maps_ref[0, 0, c, own, :], maps_ref[0, 1, c, own, :]
            else:
                real, imag = pieces[k][0, c], pieces[k][1, c]
            real, imag = real.astype(jnp.float32), imag.astype(jnp.float32)
            maps.append((real, imag))
            term_real = real * turned[k][0] - imag * turned[k][1]
            term_imag = real * turned[k][1] + imag * turned[k][0]
            fold_real = term_real if k == 0 else fold_real + term_real
            fold_imag = term_imag if k == 0 else fold_imag + term_imag
        new = []
        for k in range(FOLDS):
            real, imag = maps[k]
            new.append(sums[2 * k] + (real * fold_real + imag * fold_imag))
            new.append(sums[2 * k + 1] + (real * fold_imag - imag * fold_real))
        return tuple(new)

    zeros = tuple(jnp.zeros(offs.shape, jnp.float32) for _ in range(2 * FOLDS))
    sums = lax.fori_loop(0, coils, step, zeros, unroll=8)
    out0[0], out0[1] = 0.25 * sums[0], 0.25 * sums[1]
    results = []
    for k in range(1, FOLDS):
        real, imag = 0.25 * sums[2 * k], 0.25 * sums[2 * k + 1]
        cosine, sine = units[k]
        results.append((cosine * real + sine * imag, cosine * imag - sine * real))
    for slot, distance in enumerate(BACK):
        even, other = (results[order.index(distance)] for order in ORDERS)
        for part in range(2):
            outs[slot + 1][part] = jnp.where(odd, other[part], even[part])


def fold(stride, chunk, coil_maps, field, pieces, offs):
    coils = coil_maps.shape[2]
    _, rows, z = offs.shape
    return pl.pallas_call(
        functools.partial(fold_kernel, stride, chunk),
        in_specs=[VMEM] * 6,
        out_specs=[VMEM] * FOLDS,
        out_shape=[jax.ShapeDtypeStruct((2, rows, z), jnp.float32)] * FOLDS,
        cost_estimate=pl.CostEstimate(flops=70 * coils * rows * z, bytes_accessed=16 * coils * rows * z, transcendentals=0),
        compiler_params=pltpu.CompilerParams(vmem_limit_bytes=8 << 20),
        name="fold",
    )(coil_maps, field, *pieces, offs)


def shifted(value, lane, tap, width):
    if tap == 1:
        return value
    if tap == 0:
        return jnp.where(lane == 0, 0.0, pltpu.roll(value, 1, 1))
    return jnp.where(lane == width - 1, 0.0, pltpu.roll(value, width - 1, 1))


def denoise_kernel(stride, chunk, *refs):
    step_ref, tail_ref, field_ref, w1_ref, b1_ref, w2_ref, b2_ref, w3_ref, *normals = refs[:12]
    padded, window, low, hidden_one, hidden_two = refs[-5:]
    _, _, x_size, z = field_ref.shape
    ch = b1_ref.shape[0]
    half = x_size // 2
    cut = half - QUAD
    if chunk == 0:
        out_ref, line_ref, one_ref, two_ref = refs[12:16]
        begin, end, blank = 0, half, 0
    else:
        done_ref, line_ref, one_ref, two_ref, out_ref = refs[12:17]
        begin, end, blank = half, x_size, half - GROUP
    share, _ = place(stride)
    rows = normals[0].shape[1]
    for k, ref in enumerate(normals):
        source = share if k == 0 else share ^ BACK[k - 1]
        start = pl.multiple_of(PAD + begin + source * rows, rows)
        for part in range(2):
            padded[part, pl.ds(start, rows), :] = ref[part]
    edge = jnp.zeros((PAD, z), jnp.float32)
    for part in range(2):
        padded[part, PAD + end : PAD + end + PAD, :] = edge
        if chunk == 0:
            padded[part, 0:PAD, :] = edge
        else:
            padded[part, half - GROUP : half - GROUP + PAD, :] = edge
            padded[part, half - GROUP + PAD : half - GROUP + 2 * PAD, :] = edge
            padded[part, half : half + PAD, :] = line_ref[part]
        base = field_ref[0, part, begin:end, :]
        stepped = base - step_ref[begin:end, :] * (padded[part, PAD + begin : PAD + end, :] - base)
        padded[part, PAD + begin : PAD + end, :] = stepped
    first, last = blank, end + 2 * PAD
    lane = lax.broadcasted_iota(jnp.int32, (last - first, z), 1)
    for tap in range(3):
        for part in range(2):
            window[tap, part, first:last, :] = shifted(padded[part, first:last, :], lane, tap, z).astype(jnp.bfloat16)
    span = GROUP + 2 * PAD
    groups = range(blank // GROUP, end // GROUP)
    for g in groups:
        for tap in range(3):
            for part in range(2):
                low[(tap * 2 + part) * span : (tap * 2 + part + 1) * span, g * z : (g + 1) * z] = window[
                    tap, part, g * GROUP : g * GROUP + span, :
                ]

    def block(x, count=1):
        return slice((x + 1) * ch, (x + 1 + count) * ch)

    empty = jnp.zeros((ch, z), jnp.bfloat16)
    hidden_one[block(end)] = empty
    hidden_two[block(end)] = empty
    if chunk == 0:
        hidden_one[block(-1)] = empty
        hidden_two[block(-1)] = empty
    else:
        hidden_one[block(cut - 1, QUAD)] = one_ref[...]
        for x in range(half - GROUP - 1, cut - 1):
            hidden_two[block(x)] = empty
        hidden_two[block(cut - 1)] = two_ref[...]

    bias = b1_ref[...]
    if chunk == 1:
        g = half // GROUP - 1
        out = jnp.dot(
            w1_ref[(GROUP - 1) * ch :, :], low[:, g * z : (g + 1) * z], preferred_element_type=jnp.float32
        )
        hidden_one[block(half - 1)] = jnp.maximum(out + bias, 0.0).astype(jnp.bfloat16)
    for r in range(0, GROUP, 8):
        for g in range(begin // GROUP, end // GROUP, 2):
            out = jnp.dot(
                w1_ref[r * ch : (r + 8) * ch, :], low[:, g * z : (g + 2) * z], preferred_element_type=jnp.float32
            )
            for i in range(8):
                for j in range(2):
                    value = jnp.maximum(out[i * ch : (i + 1) * ch, j * z : (j + 1) * z] + bias, 0.0)
                    hidden_one[block((g + j) * GROUP + r + i)] = value.astype(jnp.bfloat16)

    bias = b2_ref[...]
    lane = lax.broadcasted_iota(jnp.int32, (ch, z), 1)
    start = 0 if chunk == 0 else cut
    spread = 8 if chunk == 0 else 6
    stride = (end - start) // spread
    for q in range(start, start + stride, PAIR):
        out = jnp.dot(
            w2_ref[...],
            jnp.concatenate([hidden_one[block(q + j * stride - 1, PAIR + 2)] for j in range(spread)], axis=1),
            preferred_element_type=jnp.float32,
        )
        for i in range(PAIR):
            for j in range(spread):
                total = bias
                for tap in range(3):
                    at = (tap * PAIR + i) * ch
                    total = total + shifted(out[at : at + ch, j * z : (j + 1) * z], lane, tap, z)
                hidden_two[block(q + j * stride + i)] = jnp.maximum(total, 0.0).astype(jnp.bfloat16)

    lane = lax.broadcasted_iota(jnp.int32, (2 * GROUP, z), 1)
    starts = [g * GROUP for g in groups]
    out = jnp.dot(
        w3_ref[...],
        jnp.concatenate([hidden_two[block(x - 1, GROUP + 2)] for x in starts], axis=1),
        preferred_element_type=jnp.float32,
    )
    for j, x in enumerate(starts):
        total = None
        for tap in range(3):
            part = out[tap * 2 * GROUP : (tap + 1) * 2 * GROUP, j * z : (j + 1) * z]
            part = shifted(part, lane, tap, z)
            total = part if total is None else total + part
        for part in range(2):
            value = (
                padded[part, PAD + x : PAD + x + GROUP, :]
                + total[part * GROUP : (part + 1) * GROUP]
                + tail_ref[part * GROUP : (part + 1) * GROUP, :]
            )
            if chunk == 0:
                out_ref[part, x : x + GROUP, :] = value
            elif x < half:
                keep = lax.broadcasted_iota(jnp.int32, (GROUP, z), 0) < cut - x
                out_ref[0, part, 0:x, :] = done_ref[part, 0:x, :]
                out_ref[0, part, x:half, :] = jnp.where(keep, done_ref[part, x:half, :], value)
            else:
                out_ref[0, part, x : x + GROUP, :] = value
    if chunk == 0:
        for part in range(2):
            line_ref[part] = padded[part, half : half + PAD, :]
        one_ref[...] = hidden_one[block(cut - 1, QUAD)]
        two_ref[...] = hidden_two[block(cut - 1)]


def denoise(stride, chunk, field, normals, weights, state):
    _, _, x_size, z = field.shape
    w1, b1, w2, b2, w3, tail, step = weights
    ch = b1.shape[0]
    span = GROUP + 2 * PAD
    if chunk == 0:
        out_shape = [
            jax.ShapeDtypeStruct((2, x_size // 2, z), jnp.float32),
            jax.ShapeDtypeStruct((2, PAD, z), jnp.float32),
            jax.ShapeDtypeStruct((QUAD * ch, z), jnp.bfloat16),
            jax.ShapeDtypeStruct((ch, z), jnp.bfloat16),
        ]
        out_specs = [VMEM] * 4
    else:
        out_shape = jax.ShapeDtypeStruct(field.shape, jnp.float32)
        out_specs = VMEM
    return pl.pallas_call(
        functools.partial(denoise_kernel, stride, chunk),
        in_specs=[VMEM] * (12 + len(state)),
        out_specs=out_specs,
        out_shape=out_shape,
        scratch_shapes=[
            pltpu.VMEM((2, x_size + 2 * PAD, z), jnp.float32),
            pltpu.VMEM((3, 2, x_size + 2 * PAD, z), jnp.bfloat16),
            pltpu.VMEM((6 * span, x_size // GROUP * z), jnp.bfloat16),
            pltpu.VMEM(((x_size + 2) * ch, z), jnp.bfloat16),
            pltpu.VMEM(((x_size + 2) * ch, z), jnp.bfloat16),
        ],
        cost_estimate=pl.CostEstimate(flops=2_000_000_000, bytes_accessed=2_000_000, transcendentals=0),
        compiler_params=pltpu.CompilerParams(vmem_limit_bytes=16 << 20),
        name=("denoise_first", "denoise_rest")[chunk],
    )(step, tail, field, w1, b1, w2, b2, w3, *normals, *state)


def prepare_kernel(
    w_in_ref, b_in_ref, w_mid_ref, b_mid_ref, w_out_ref, b_out_ref, step_in_ref,
    w1_ref, b1_ref, w2_ref, b2_ref, w3_ref, tail_ref, step_ref,
):
    ch, z = b1_ref.shape
    span = GROUP + 2 * PAD
    step_ref[...] = jnp.full(step_ref.shape, step_in_ref[0])
    for part in range(2):
        tail_ref[part * GROUP : (part + 1) * GROUP, :] = jnp.full((GROUP, z), b_out_ref[part])
    b1_ref[...] = jnp.transpose(jnp.broadcast_to(b_in_ref[...], (z, ch)))
    b2_ref[...] = jnp.transpose(jnp.broadcast_to(b_mid_ref[...], (z, ch)))
    taps = w_in_ref[...]
    row = lax.broadcasted_iota(jnp.int32, (18, 6 * span), 0)
    column = lax.broadcasted_iota(jnp.int32, (18, 6 * span), 1)
    place = (row % 6) * span + row // 6 + (PAD - 1)
    for r in range(GROUP):
        select = jnp.where(column == place + r, 1.0, 0.0).astype(jnp.bfloat16)
        w1_ref[r * ch : (r + 1) * ch, :] = lax.dot_general(
            taps, select, (((0,), (0,)), ((), ())), preferred_element_type=jnp.float32
        ).astype(jnp.bfloat16)
    w2_ref[...] = jnp.zeros_like(w2_ref)
    for dz in range(3):
        for dx in range(3):
            block = w_mid_ref[dx, dz]
            for r in range(PAIR):
                first = (dz * PAIR + r) * ch
                w2_ref[first : first + ch, (r + dx) * ch : (r + dx + 1) * ch] = block
    wide = (GROUP, (GROUP + 2) * ch)
    offset = lax.broadcasted_iota(jnp.int32, wide, 1) // ch - lax.broadcasted_iota(jnp.int32, wide, 0)
    for dz in range(3):
        for part in range(2):
            total = jnp.zeros(wide, jnp.float32)
            for dx in range(3):
                line = w_out_ref[dx, dz, part : part + 1, :].astype(jnp.float32)
                line = jnp.concatenate([line] * (GROUP + 2), axis=1)
                total = jnp.where(offset == dx, jnp.broadcast_to(line, wide), total)
            first = (dz * 2 + part) * GROUP
            w3_ref[first : first + GROUP, :] = total.astype(jnp.bfloat16)


def prepare(w_in, b_in, w_mid, b_mid, w_out, b_out, step, x_size, z):
    ch = w_mid.shape[0]
    shapes = [
        jax.ShapeDtypeStruct((GROUP * ch, 6 * (GROUP + 2 * PAD)), jnp.bfloat16),
        jax.ShapeDtypeStruct((ch, z), jnp.float32),
        jax.ShapeDtypeStruct((3 * PAIR * ch, (PAIR + 2) * ch), jnp.bfloat16),
        jax.ShapeDtypeStruct((ch, z), jnp.float32),
        jax.ShapeDtypeStruct((6 * GROUP, (GROUP + 2) * ch), jnp.bfloat16),
        jax.ShapeDtypeStruct((2 * GROUP, z), jnp.float32),
        jax.ShapeDtypeStruct((x_size, z), jnp.float32),
    ]
    return pl.pallas_call(
        prepare_kernel,
        in_specs=[VMEM] * 5 + [SMEM] * 2,
        out_specs=[VMEM] * 7,
        out_shape=shapes,
        cost_estimate=pl.CostEstimate(flops=1_000_000_000, bytes_accessed=8_000_000, transcendentals=0),
        compiler_params=pltpu.CompilerParams(vmem_limit_bytes=8 << 20),
        name="prepare",
    )(
        w_in.transpose(2, 3, 1, 0).reshape(18, ch),
        b_in[None],
        w_mid.transpose(2, 3, 0, 1),
        b_mid[None],
        w_out.transpose(2, 3, 0, 1),
        b_out,
        step,
    )


def pack_kernel(stride, maps_ref, field_ref, *refs):
    outs, (held, sems, field_sem) = refs[:-3], refs[-3:]
    coils = maps_ref.shape[2]
    rows = outs[-1].shape[2]
    share, distances = place(stride)
    field_copy = pltpu.make_async_copy(field_ref.at[0], held, field_sem)
    field_copy.start()
    copies = []
    spans = []
    for ref, (i, chunks) in zip(outs, SENT):
        for at, chunk in enumerate(chunks):
            first = pl.multiple_of((chunk * FOLDS + (share ^ distances[i])) * rows, rows)
            here, there = pl.ds(first, rows), pl.ds(at * rows, rows)
            spans.append((ref, here, there))
            for part in range(2):
                copy = pltpu.make_async_copy(
                    maps_ref.at[0, part, :, here, :], ref.at[part, 0:coils, there, :], sems.at[len(copies)]
                )
                copy.start()
                copies.append(copy)
    field_copy.wait()
    for ref, here, there in spans:
        for part in range(2):
            value = held[part, here, :]
            high = value.astype(jnp.bfloat16)
            ref[part, coils, there, :] = high
            ref[part, coils + 1, there, :] = (value - high.astype(jnp.float32)).astype(jnp.bfloat16)
    for copy in copies:
        copy.wait()


def pack(stride, coil_maps, field):
    _, _, coils, x_size, z = coil_maps.shape
    rows = x_size // FOLDS // CHUNKS
    pieces = [jax.ShapeDtypeStruct((2, coils + 2, len(chunks) * rows, z), jnp.bfloat16) for _, chunks in SENT]
    return pl.pallas_call(
        functools.partial(pack_kernel, stride),
        in_specs=[HBM, HBM],
        out_specs=[VMEM] * len(pieces),
        out_shape=pieces,
        scratch_shapes=[
            pltpu.VMEM((2, x_size, z), jnp.float32),
            pltpu.SemaphoreType.DMA((2 * sum(len(chunks) for _, chunks in SENT),)),
            pltpu.SemaphoreType.DMA,
        ],
        cost_estimate=pl.CostEstimate(flops=0, bytes_accessed=2_000_000, transcendentals=0),
        compiler_params=pltpu.CompilerParams(vmem_limit_bytes=PACK_LIMIT),
        name="pack",
    )(*(pltpu.with_memory_space_constraint(array, pltpu.HBM) for array in (coil_maps, field)))


def per_device(zero_filled, coil_maps, offsets, step_sizes, w_in, b_in, w_mid, b_mid, w_out, b_out):
    devices = lax.axis_size("gy")
    stride = devices // FOLDS
    x_size, z = zero_filled.shape[2:]
    rows = x_size // FOLDS // CHUNKS
    share = lax.axis_index("gy") // stride

    def trade(value, distances):
        pairs = [(j, (j // stride ^ distances[j % 2]) * stride + j % stride) for j in range(devices)]
        return lax.ppermute(value, "gy", pairs)

    sent = pack(stride, coil_maps, zero_filled)
    pieces = [trade(value, [order[i] for order in ORDERS]) for value, (i, _) in zip(sent, SENT)]
    chunks = [
        [next(piece for piece, (j, held) in zip(pieces, SENT) if i == j and chunk in held) for i in range(FOLDS - 1)]
        for chunk in range(CHUNKS)
    ]
    weights = prepare(w_in, b_in, w_mid, b_mid, w_out, b_out, step_sizes, x_size, z)
    offs = lax.dynamic_index_in_dim(offsets.reshape(CHUNKS, FOLDS, rows), share, 1, keepdims=False)
    offs = jnp.broadcast_to(offs[:, :, None], (CHUNKS, rows, z))
    chunks[0], weights, offs = lax.optimization_barrier((chunks[0], weights, offs))
    first = fold(stride, 0, coil_maps, zero_filled, chunks[0], offs)
    first = [first[0]] + [trade(value, (k, k)) for value, k in zip(first[1:], BACK)]
    rest = fold(stride, 1, coil_maps, zero_filled, chunks[1], offs)
    back = [trade(value, (k, k)) for value, k in zip(rest[1:], BACK)]
    first, own = lax.optimization_barrier((first, rest[0]))
    state = denoise(stride, 0, zero_filled, first, weights, [])
    return denoise(stride, 1, zero_filled, [own] + back, weights, state)


def solution(mesh):
    in_specs = (
        P(("parts", "gy"), None, None, None),
        P(("parts", "gy"), None, None, None, None),
        P("parts"),
        P(),
        P(),
        P(),
        P(),
        P(),
        P(),
        P(),
    )
    out_specs = P(("parts", "gy"), None, None, None)
    return jax.shard_map(
        per_device, mesh=mesh, in_specs=in_specs, out_specs=out_specs, check_vma=False
    )
```

```python
import functools

import jax
import jax.numpy as jnp
from jax import lax
from jax.experimental import pallas as pl
from jax.experimental.pallas import tpu as pltpu
from jax.sharding import PartitionSpec as P

FOLDS = 4
GROUP = 16
QUAD = 4
PAIR = 2
PAD = 8
ORDERS = ((1, 2, 3), (3, 1, 2))
BACK = (3, 2, 1)
PACK_LIMIT = 8 << 20
CHUNKS = 2
SENT = ((0, (0, 1)), (1, (0,)), (2, (0,)), (1, (1,)), (2, (1,)))

VMEM = pl.BlockSpec(memory_space=pltpu.VMEM)
HBM = pl.BlockSpec(memory_space=pltpu.HBM)
SMEM = pl.BlockSpec(memory_space=pltpu.SMEM)


def place(stride):
    position = lax.axis_index("gy")
    odd = position % 2
    return position // stride, [jnp.where(odd == 0, even, other) for even, other in zip(*ORDERS)]


def fold_kernel(stride, chunk, maps_ref, field_ref, one_ref, two_ref, three_ref, offs_ref, out0, out1, out2, out3):
    coils = maps_ref.shape[2]
    rows = out0.shape[1]
    share, distances = place(stride)
    odd = distances[0] != ORDERS[0][0]
    own = pl.ds(pl.multiple_of((chunk * FOLDS + share) * rows, rows), rows)
    offs = offs_ref[chunk]
    pieces = (None, one_ref.at[:, :, pl.ds(chunk * rows, rows), :], two_ref, three_ref)
    outs = (out0, out1, out2, out3)
    turned = []
    units = []
    for k in range(FOLDS):
        if k == 0:
            real, imag = field_ref[0, 0, own, :], field_ref[0, 1, own, :]
            turned.append((real, imag))
            units.append(None)
            continue
        piece = pieces[k]
        real = piece[0, coils].astype(jnp.float32) + piece[0, coils + 1].astype(jnp.float32)
        imag = piece[1, coils].astype(jnp.float32) + piece[1, coils + 1].astype(jnp.float32)
        turns = (((share ^ distances[k - 1]) - share) * offs) & 3
        zero, one = jnp.zeros_like(real), jnp.ones_like(real)
        cosine = jnp.where(turns == 0, one, jnp.where(turns == 2, -one, zero))
        sine = jnp.where(turns == 3, one, jnp.where(turns == 1, -one, zero))
        units.append((cosine, sine))
        turned.append((cosine * real - sine * imag, cosine * imag + sine * real))

    def step(c, sums):
        maps = []
        fold_real = fold_imag = None
        for k in range(FOLDS):
            if k == 0:
                real, imag = maps_ref[0, 0, c, own, :], maps_ref[0, 1, c, own, :]
            else:
                real, imag = pieces[k][0, c], pieces[k][1, c]
            real, imag = real.astype(jnp.float32), imag.astype(jnp.float32)
            maps.append((real, imag))
            term_real = real * turned[k][0] - imag * turned[k][1]
            term_imag = real * turned[k][1] + imag * turned[k][0]
            fold_real = term_real if k == 0 else fold_real + term_real
            fold_imag = term_imag if k == 0 else fold_imag + term_imag
        new = []
        for k in range(FOLDS):
            real, imag = maps[k]
            new.append(sums[2 * k] + (real * fold_real + imag * fold_imag))
            new.append(sums[2 * k + 1] + (real * fold_imag - imag * fold_real))
        return tuple(new)

    zeros = tuple(jnp.zeros(offs.shape, jnp.float32) for _ in range(2 * FOLDS))
    sums = lax.fori_loop(0, coils, step, zeros, unroll=8)
    out0[0], out0[1] = 0.25 * sums[0], 0.25 * sums[1]
    results = []
    for k in range(1, FOLDS):
        real, imag = 0.25 * sums[2 * k], 0.25 * sums[2 * k + 1]
        cosine, sine = units[k]
        results.append((cosine * real + sine * imag, cosine * imag - sine * real))
    for slot, distance in enumerate(BACK):
        even, other = (results[order.index(distance)] for order in ORDERS)
        for part in range(2):
            outs[slot + 1][part] = jnp.where(odd, other[part], even[part])


def fold(stride, chunk, coil_maps, field, pieces, offs):
    coils = coil_maps.shape[2]
    _, rows, z = offs.shape
    return pl.pallas_call(
        functools.partial(fold_kernel, stride, chunk),
        in_specs=[VMEM] * 6,
        out_specs=[VMEM] * FOLDS,
        out_shape=[jax.ShapeDtypeStruct((2, rows, z), jnp.float32)] * FOLDS,
        cost_estimate=pl.CostEstimate(flops=70 * coils * rows * z, bytes_accessed=16 * coils * rows * z, transcendentals=0),
        compiler_params=pltpu.CompilerParams(vmem_limit_bytes=8 << 20),
        name="fold",
    )(coil_maps, field, *pieces, offs)


def shifted(value, lane, tap, width):
    if tap == 1:
        return value
    if tap == 0:
        return jnp.where(lane == 0, 0.0, pltpu.roll(value, 1, 1))
    return jnp.where(lane == width - 1, 0.0, pltpu.roll(value, width - 1, 1))


def denoise_kernel(stride, chunk, *refs):
    step_ref, tail_ref, field_ref, w1_ref, b1_ref, w2_ref, b2_ref, w3_ref, *normals = refs[:12]
    padded, window, low, hidden_one, hidden_two = refs[-5:]
    _, _, x_size, z = field_ref.shape
    ch = b1_ref.shape[0]
    half = x_size // 2
    cut = half - QUAD
    if chunk == 0:
        out_ref, line_ref, one_ref, two_ref = refs[12:16]
        begin, end, blank = 0, half, 0
    else:
        done_ref, line_ref, one_ref, two_ref, out_ref = refs[12:17]
        begin, end, blank = half, x_size, half - GROUP
    share, _ = place(stride)
    rows = normals[0].shape[1]
    for k, ref in enumerate(normals):
        source = share if k == 0 else share ^ BACK[k - 1]
        start = pl.multiple_of(PAD + begin + source * rows, rows)
        for part in range(2):
            padded[part, pl.ds(start, rows), :] = ref[part]
    edge = jnp.zeros((PAD, z), jnp.float32)
    for part in range(2):
        padded[part, PAD + end : PAD + end + PAD, :] = edge
        if chunk == 0:
            padded[part, 0:PAD, :] = edge
        else:
            padded[part, half - GROUP : half - GROUP + PAD, :] = edge
            padded[part, half - GROUP + PAD : half - GROUP + 2 * PAD, :] = edge
            padded[part, half : half + PAD, :] = line_ref[part]
        base = field_ref[0, part, begin:end, :]
        stepped = base - step_ref[begin:end, :] * (padded[part, PAD + begin : PAD + end, :] - base)
        padded[part, PAD + begin : PAD + end, :] = stepped
    first, last = blank, end + 2 * PAD
    lane = lax.broadcasted_iota(jnp.int32, (last - first, z), 1)
    for tap in range(3):
        for part in range(2):
            window[tap, part, first:last, :] = shifted(padded[part, first:last, :], lane, tap, z).astype(jnp.bfloat16)
    span = GROUP + 2 * PAD
    groups = range(blank // GROUP, end // GROUP)
    for g in groups:
        for tap in range(3):
            for part in range(2):
                low[(tap * 2 + part) * span : (tap * 2 + part + 1) * span, g * z : (g + 1) * z] = window[
                    tap, part, g * GROUP : g * GROUP + span, :
                ]

    def block(x, count=1):
        return slice((x + 1) * ch, (x + 1 + count) * ch)

    empty = jnp.zeros((ch, z), jnp.bfloat16)
    hidden_one[block(end)] = empty
    hidden_two[block(end)] = empty
    if chunk == 0:
        hidden_one[block(-1)] = empty
        hidden_two[block(-1)] = empty
    else:
        hidden_one[block(cut - 1, QUAD)] = one_ref[...]
        for x in range(half - GROUP - 1, cut - 1):
            hidden_two[block(x)] = empty
        hidden_two[block(cut - 1)] = two_ref[...]

    bias = b1_ref[...]
    if chunk == 1:
        g = half // GROUP - 1
        out = jnp.dot(
            w1_ref[(GROUP - 1) * ch :, :], low[:, g * z : (g + 1) * z], preferred_element_type=jnp.float32
        )
        hidden_one[block(half - 1)] = jnp.maximum(out + bias, 0.0).astype(jnp.bfloat16)
    for r in range(0, GROUP, QUAD):
        for g in range(begin // GROUP, end // GROUP, 2):
            out = jnp.dot(
                w1_ref[r * ch : (r + QUAD) * ch, :], low[:, g * z : (g + 2) * z], preferred_element_type=jnp.float32
            )
            for i in range(QUAD):
                for j in range(2):
                    value = jnp.maximum(out[i * ch : (i + 1) * ch, j * z : (j + 1) * z] + bias, 0.0)
                    hidden_one[block((g + j) * GROUP + r + i)] = value.astype(jnp.bfloat16)

    bias = b2_ref[...]
    lane = lax.broadcasted_iota(jnp.int32, (ch, z), 1)
    start = 0 if chunk == 0 else cut
    stride = (end - start) // 2
    for q in range(start, start + stride, PAIR):
        out = jnp.dot(
            w2_ref[...],
            jnp.concatenate([hidden_one[block(q - 1, PAIR + 2)], hidden_one[block(q + stride - 1, PAIR + 2)]], axis=1),
            preferred_element_type=jnp.float32,
        )
        for i in range(PAIR):
            for j in range(2):
                total = bias
                for tap in range(3):
                    at = (tap * PAIR + i) * ch
                    total = total + shifted(out[at : at + ch, j * z : (j + 1) * z], lane, tap, z)
                hidden_two[block(q + j * stride + i)] = jnp.maximum(total, 0.0).astype(jnp.bfloat16)

    lane = lax.broadcasted_iota(jnp.int32, (2 * GROUP, z), 1)
    starts = [g * GROUP for g in groups]
    out = jnp.dot(
        w3_ref[...],
        jnp.concatenate([hidden_two[block(x - 1, GROUP + 2)] for x in starts], axis=1),
        preferred_element_type=jnp.float32,
    )
    for j, x in enumerate(starts):
        total = None
        for tap in range(3):
            part = out[tap * 2 * GROUP : (tap + 1) * 2 * GROUP, j * z : (j + 1) * z]
            part = shifted(part, lane, tap, z)
            total = part if total is None else total + part
        for part in range(2):
            value = (
                padded[part, PAD + x : PAD + x + GROUP, :]
                + total[part * GROUP : (part + 1) * GROUP]
                + tail_ref[part * GROUP : (part + 1) * GROUP, :]
            )
            if chunk == 0:
                out_ref[part, x : x + GROUP, :] = value
            elif x < half:
                keep = lax.broadcasted_iota(jnp.int32, (GROUP, z), 0) < cut - x
                out_ref[0, part, 0:x, :] = done_ref[part, 0:x, :]
                out_ref[0, part, x:half, :] = jnp.where(keep, done_ref[part, x:half, :], value)
            else:
                out_ref[0, part, x : x + GROUP, :] = value
    if chunk == 0:
        for part in range(2):
            line_ref[part] = padded[part, half : half + PAD, :]
        one_ref[...] = hidden_one[block(cut - 1, QUAD)]
        two_ref[...] = hidden_two[block(cut - 1)]


def denoise(stride, chunk, field, normals, weights, state):
    _, _, x_size, z = field.shape
    w1, b1, w2, b2, w3, tail, step = weights
    ch = b1.shape[0]
    span = GROUP + 2 * PAD
    if chunk == 0:
        out_shape = [
            jax.ShapeDtypeStruct((2, x_size // 2, z), jnp.float32),
            jax.ShapeDtypeStruct((2, PAD, z), jnp.float32),
            jax.ShapeDtypeStruct((QUAD * ch, z), jnp.bfloat16),
            jax.ShapeDtypeStruct((ch, z), jnp.bfloat16),
        ]
        out_specs = [VMEM] * 4
    else:
        out_shape = jax.ShapeDtypeStruct(field.shape, jnp.float32)
        out_specs = VMEM
    return pl.pallas_call(
        functools.partial(denoise_kernel, stride, chunk),
        in_specs=[VMEM] * (12 + len(state)),
        out_specs=out_specs,
        out_shape=out_shape,
        scratch_shapes=[
            pltpu.VMEM((2, x_size + 2 * PAD, z), jnp.float32),
            pltpu.VMEM((3, 2, x_size + 2 * PAD, z), jnp.bfloat16),
            pltpu.VMEM((6 * span, x_size // GROUP * z), jnp.bfloat16),
            pltpu.VMEM(((x_size + 2) * ch, z), jnp.bfloat16),
            pltpu.VMEM(((x_size + 2) * ch, z), jnp.bfloat16),
        ],
        cost_estimate=pl.CostEstimate(flops=2_000_000_000, bytes_accessed=2_000_000, transcendentals=0),
        compiler_params=pltpu.CompilerParams(vmem_limit_bytes=16 << 20),
        name=("denoise_first", "denoise_rest")[chunk],
    )(step, tail, field, w1, b1, w2, b2, w3, *normals, *state)


def prepare_kernel(
    w_in_ref, b_in_ref, w_mid_ref, b_mid_ref, w_out_ref, b_out_ref, step_in_ref,
    w1_ref, b1_ref, w2_ref, b2_ref, w3_ref, tail_ref, step_ref,
):
    ch, z = b1_ref.shape
    span = GROUP + 2 * PAD
    step_ref[...] = jnp.full(step_ref.shape, step_in_ref[0])
    for part in range(2):
        tail_ref[part * GROUP : (part + 1) * GROUP, :] = jnp.full((GROUP, z), b_out_ref[part])
    b1_ref[...] = jnp.transpose(jnp.broadcast_to(b_in_ref[...], (z, ch)))
    b2_ref[...] = jnp.transpose(jnp.broadcast_to(b_mid_ref[...], (z, ch)))
    taps = w_in_ref[...]
    row = lax.broadcasted_iota(jnp.int32, (18, 6 * span), 0)
    column = lax.broadcasted_iota(jnp.int32, (18, 6 * span), 1)
    place = (row % 6) * span + row // 6 + (PAD - 1)
    for r in range(GROUP):
        select = jnp.where(column == place + r, 1.0, 0.0).astype(jnp.bfloat16)
        w1_ref[r * ch : (r + 1) * ch, :] = lax.dot_general(
            taps, select, (((0,), (0,)), ((), ())), preferred_element_type=jnp.float32
        ).astype(jnp.bfloat16)
    w2_ref[...] = jnp.zeros_like(w2_ref)
    for dz in range(3):
        for dx in range(3):
            block = w_mid_ref[dx, dz]
            for r in range(PAIR):
                first = (dz * PAIR + r) * ch
                w2_ref[first : first + ch, (r + dx) * ch : (r + dx + 1) * ch] = block
    wide = (GROUP, (GROUP + 2) * ch)
    offset = lax.broadcasted_iota(jnp.int32, wide, 1) // ch - lax.broadcasted_iota(jnp.int32, wide, 0)
    for dz in range(3):
        for part in range(2):
            total = jnp.zeros(wide, jnp.float32)
            for dx in range(3):
                line = w_out_ref[dx, dz, part : part + 1, :].astype(jnp.float32)
                line = jnp.concatenate([line] * (GROUP + 2), axis=1)
                total = jnp.where(offset == dx, jnp.broadcast_to(line, wide), total)
            first = (dz * 2 + part) * GROUP
            w3_ref[first : first + GROUP, :] = total.astype(jnp.bfloat16)


def prepare(w_in, b_in, w_mid, b_mid, w_out, b_out, step, x_size, z):
    ch = w_mid.shape[0]
    shapes = [
        jax.ShapeDtypeStruct((GROUP * ch, 6 * (GROUP + 2 * PAD)), jnp.bfloat16),
        jax.ShapeDtypeStruct((ch, z), jnp.float32),
        jax.ShapeDtypeStruct((3 * PAIR * ch, (PAIR + 2) * ch), jnp.bfloat16),
        jax.ShapeDtypeStruct((ch, z), jnp.float32),
        jax.ShapeDtypeStruct((6 * GROUP, (GROUP + 2) * ch), jnp.bfloat16),
        jax.ShapeDtypeStruct((2 * GROUP, z), jnp.float32),
        jax.ShapeDtypeStruct((x_size, z), jnp.float32),
    ]
    return pl.pallas_call(
        prepare_kernel,
        in_specs=[VMEM] * 5 + [SMEM] * 2,
        out_specs=[VMEM] * 7,
        out_shape=shapes,
        cost_estimate=pl.CostEstimate(flops=1_000_000_000, bytes_accessed=8_000_000, transcendentals=0),
        compiler_params=pltpu.CompilerParams(vmem_limit_bytes=8 << 20),
        name="prepare",
    )(
        w_in.transpose(2, 3, 1, 0).reshape(18, ch),
        b_in[None],
        w_mid.transpose(2, 3, 0, 1),
        b_mid[None],
        w_out.transpose(2, 3, 0, 1),
        b_out,
        step,
    )


def pack_kernel(stride, maps_ref, field_ref, *refs):
    outs, (held, sems, field_sem) = refs[:-3], refs[-3:]
    coils = maps_ref.shape[2]
    rows = outs[-1].shape[2]
    share, distances = place(stride)
    field_copy = pltpu.make_async_copy(field_ref.at[0], held, field_sem)
    field_copy.start()
    copies = []
    spans = []
    for ref, (i, chunks) in zip(outs, SENT):
        for at, chunk in enumerate(chunks):
            first = pl.multiple_of((chunk * FOLDS + (share ^ distances[i])) * rows, rows)
            here, there = pl.ds(first, rows), pl.ds(at * rows, rows)
            spans.append((ref, here, there))
            for part in range(2):
                copy = pltpu.make_async_copy(
                    maps_ref.at[0, part, :, here, :], ref.at[part, 0:coils, there, :], sems.at[len(copies)]
                )
                copy.start()
                copies.append(copy)
    field_copy.wait()
    for ref, here, there in spans:
        for part in range(2):
            value = held[part, here, :]
            high = value.astype(jnp.bfloat16)
            ref[part, coils, there, :] = high
            ref[part, coils + 1, there, :] = (value - high.astype(jnp.float32)).astype(jnp.bfloat16)
    for copy in copies:
        copy.wait()


def pack(stride, coil_maps, field):
    _, _, coils, x_size, z = coil_maps.shape
    rows = x_size // FOLDS // CHUNKS
    pieces = [jax.ShapeDtypeStruct((2, coils + 2, len(chunks) * rows, z), jnp.bfloat16) for _, chunks in SENT]
    return pl.pallas_call(
        functools.partial(pack_kernel, stride),
        in_specs=[HBM, HBM],
        out_specs=[VMEM] * len(pieces),
        out_shape=pieces,
        scratch_shapes=[
            pltpu.VMEM((2, x_size, z), jnp.float32),
            pltpu.SemaphoreType.DMA((2 * sum(len(chunks) for _, chunks in SENT),)),
            pltpu.SemaphoreType.DMA,
        ],
        cost_estimate=pl.CostEstimate(flops=0, bytes_accessed=2_000_000, transcendentals=0),
        compiler_params=pltpu.CompilerParams(vmem_limit_bytes=PACK_LIMIT),
        name="pack",
    )(*(pltpu.with_memory_space_constraint(array, pltpu.HBM) for array in (coil_maps, field)))


def per_device(zero_filled, coil_maps, offsets, step_sizes, w_in, b_in, w_mid, b_mid, w_out, b_out):
    devices = lax.axis_size("gy")
    stride = devices // FOLDS
    x_size, z = zero_filled.shape[2:]
    rows = x_size // FOLDS // CHUNKS
    share = lax.axis_index("gy") // stride

    def trade(value, distances):
        pairs = [(j, (j // stride ^ distances[j % 2]) * stride + j % stride) for j in range(devices)]
        return lax.ppermute(value, "gy", pairs)

    sent = pack(stride, coil_maps, zero_filled)
    pieces = [trade(value, [order[i] for order in ORDERS]) for value, (i, _) in zip(sent, SENT)]
    chunks = [
        [next(piece for piece, (j, held) in zip(pieces, SENT) if i == j and chunk in held) for i in range(FOLDS - 1)]
        for chunk in range(CHUNKS)
    ]
    weights = prepare(w_in, b_in, w_mid, b_mid, w_out, b_out, step_sizes, x_size, z)
    offs = lax.dynamic_index_in_dim(offsets.reshape(CHUNKS, FOLDS, rows), share, 1, keepdims=False)
    offs = jnp.broadcast_to(offs[:, :, None], (CHUNKS, rows, z))
    chunks[0], weights, offs = lax.optimization_barrier((chunks[0], weights, offs))
    first = fold(stride, 0, coil_maps, zero_filled, chunks[0], offs)
    first = [first[0]] + [trade(value, (k, k)) for value, k in zip(first[1:], BACK)]
    rest = fold(stride, 1, coil_maps, zero_filled, chunks[1], offs)
    back = [trade(value, (k, k)) for value, k in zip(rest[1:], BACK)]
    first, own = lax.optimization_barrier((first, rest[0]))
    state = denoise(stride, 0, zero_filled, first, weights, [])
    return denoise(stride, 1, zero_filled, [own] + back, weights, state)


def solution(mesh):
    in_specs = (
        P(("parts", "gy"), None, None, None),
        P(("parts", "gy"), None, None, None, None),
        P("parts"),
        P(),
        P(),
        P(),
        P(),
        P(),
        P(),
        P(),
    )
    out_specs = P(("parts", "gy"), None, None, None)
    return jax.shard_map(
        per_device, mesh=mesh, in_specs=in_specs, out_specs=out_specs, check_vma=False
    )
```
